256 devices in a mesh: dp: 8 (over z), seq: 32 (over y, x, core).
Axes of the slice: x: 4, y: 4, z: 8, core: 2. Of those that a mesh axis runs over, the one named last changes fastest.
Arguments:
- latents: bfloat16 [16, 16384, 1152], P('dp', 'seq'), may hold values from -56 to 56
- out_grad: bfloat16 [16, 16384, 1152], P('dp', 'seq'), may hold values from -6 to 6
- phrases: bfloat16 [16, 32, 1152], P('dp'), may hold values from -6 to 6
- query_weight: bfloat16 [1152, 1152], replicated, may hold values from -0.1875 to 0.1875
- key_weight: bfloat16 [1152, 1152], P('seq'), may hold values from -0.1875 to 0.1875
- value_weight: bfloat16 [1152, 1152], P('seq'), may hold values from -0.1875 to 0.1875
- first_weight: bfloat16 [1152, 1152], P('seq'), may hold values from -0.1875 to 0.1875
- second_weight: bfloat16 [1152, 1152], P('seq'), may hold values from -0.1875 to 0.1875
- region_first: int32 [16, 32], P('dp'), may hold values from 0 to 127, as said below
- region_last: int32 [16, 32], P('dp'), may hold values from 0 to 127
- phrase_counts: int32 [16], P('dp'), may hold values from 8 to 32, as said below
Outputs:
- latent_grad: bfloat16 [16, 16384, 1152], P('dp', 'seq')
- phrase_grad: bfloat16 [16, 32, 1152], P('dp')
- first_grad: float32 [1152, 1152], P('seq')
- second_grad: float32 [1152, 1152], P('seq')
The draws below stay inside these ranges and needn't reach their ends.
Inputs may be any that keep to these rules, and one draw needn't show every extreme that they name: region_first <= region_last for every phrase; phrase 0 of every image covers all 128 blocks. Slots from phrase_counts on are padding.
All inputs are finite; a program needn't handle non-finite values.
Results may differ from the reference program's by a relative error of at most 0.015.
The reference program's roundings to bfloat16 on the way (of `hidden`, `encoded`, `queries`, `probs_low`, `score_grad`, `query_grad`, `encoded_grad` and `act_grad`) count: a program that leaves them out, or rounds other values in their place, can miss the bound.
Values may be sent and summed in bfloat16 or wider, within the bound.
A program may use at most 128 MiB of HBM per device.

```python
import jax
import jax.numpy as jnp
from jax import lax

D = 1152
H = 16
HD = 72
P_SIZE = 32
BLOCK = 128
NBLK = 128
TOKENS = 16384
IMAGES = 16


def region_bounds(key):
    base_key = jax.random.fold_in(key, 41)
    start_key, span_key = jax.random.split(base_key)
    region_first = jax.random.randint(start_key, (IMAGES, P_SIZE), 0, NBLK, dtype=jnp.int32)
    levels = NBLK.bit_length()
    exponent = jax.random.randint(span_key, (IMAGES, P_SIZE), 0, levels, dtype=jnp.int32)
    span_len = jnp.left_shift(jnp.ones((IMAGES, P_SIZE), jnp.int32), exponent)
    region_last = jnp.minimum(region_first + span_len - 1, NBLK - 1)
    region_first = region_first.at[:, 0].set(0)
    region_last = region_last.at[:, 0].set(NBLK - 1)
    return (region_first, region_last)


def draw_region_first(key, part):
    return region_bounds(key)[0]


def draw_region_last(key, part):
    return region_bounds(key)[1]


def draw_phrase_counts(key, part):
    drawn = jax.random.randint(jax.random.fold_in(key, 43), (IMAGES,), P_SIZE // 4, P_SIZE + 1, dtype=jnp.int32)
    return drawn.at[0].set(P_SIZE)


def draw_latents(key, part):
    normal_key = jax.random.fold_in(jax.random.fold_in(key, 47), 0)
    drawn = jnp.clip(jax.random.normal(normal_key, (IMAGES, TOKENS, D), jnp.float32), -6.0, 6.0)
    return drawn.astype(jnp.bfloat16)


def block_scale(own_key, shape, cuts, low, largest):
    gain, own = 1.0, jax.random.fold_in(own_key, 6)
    for dim, parts in cuts:
        draws = jnp.exp(jax.random.uniform(jax.random.fold_in(own, dim), (parts,), jnp.float32, low / len(cuts), largest / len(cuts)))
        gain = gain * jnp.repeat(draws, shape[dim] // parts).reshape([-1 if axis == dim else 1 for axis in range(len(shape))])
    return gain


def gaussian(key, shape, scale, limit, shards=(), kind=jnp.bfloat16):
    gain = block_scale(key, shape, shards, -0.22, 0.18) if shards else 1.0
    result = jax.random.normal(key, shape, jnp.float32) * scale * gain
    return jnp.minimum(jnp.maximum(result, -limit), limit).astype(kind)


def setup_inputs(seed: int = 0) -> dict:
    keys = jax.random.split(jax.random.key(seed), 12)
    latents = draw_latents(jax.random.fold_in(keys[11], 71), 0)
    out_grad = gaussian(keys[1], (IMAGES, TOKENS, D), 1.0, 6.0, ((0, 8), (1, 32)))
    phrases = gaussian(keys[2], (IMAGES, P_SIZE, D), 1.0, 6.0, ((0, 8),))
    query_weight = gaussian(keys[3], (D, D), D ** -0.5, 0.1875)
    key_weight = gaussian(keys[4], (D, D), D ** -0.5, 0.1875, ((0, 32),))
    value_weight = gaussian(keys[5], (D, D), D ** -0.5, 0.1875, ((0, 32),))
    first_weight = gaussian(keys[6], (D, D), D ** -0.5, 0.1875, ((0, 32),))
    second_weight = gaussian(keys[7], (D, D), D ** -0.5, 0.1875, ((0, 32),))
    region_first = draw_region_first(jax.random.fold_in(keys[11], 71), 0)
    region_last = draw_region_last(jax.random.fold_in(keys[11], 71), 0)
    phrase_counts = draw_phrase_counts(jax.random.fold_in(keys[11], 71), 0)
    return {"latents": latents, "out_grad": out_grad, "phrases": phrases, "query_weight": query_weight, "key_weight": key_weight, "value_weight": value_weight, "first_weight": first_weight, "second_weight": second_weight, "region_first": region_first, "region_last": region_last, "phrase_counts": phrase_counts}


def silu_slope(pre_act):
    sigmoid = jax.nn.sigmoid(pre_act)
    return sigmoid * (1.0 + pre_act * (1.0 - sigmoid))


def reference(latents, out_grad, phrases, query_weight, key_weight, value_weight, first_weight, second_weight, region_first, region_last, phrase_counts):
    score_scale = HD ** -0.5
    phrase_rows = phrases.reshape(IMAGES * P_SIZE, D)
    pre_act = jnp.dot(phrase_rows, first_weight, preferred_element_type=jnp.float32)
    hidden = jax.nn.silu(pre_act).astype(jnp.bfloat16)
    encoded = jnp.dot(hidden, second_weight, preferred_element_type=jnp.float32).astype(jnp.bfloat16)
    key_rows = jnp.dot(encoded, key_weight, preferred_element_type=jnp.float32).astype(jnp.bfloat16)
    value_rows = jnp.dot(encoded, value_weight, preferred_element_type=jnp.float32).astype(jnp.bfloat16)
    block_ids = jnp.arange(TOKENS, dtype=jnp.int32) // BLOCK
    phrase_ids = jnp.arange(P_SIZE, dtype=jnp.int32)
    best = lax.Precision.HIGHEST

    def one_image(inputs):
        image_latents, image_grad, image_keys, image_values, first_block, last_block, count = inputs
        queries = jnp.dot(image_latents, query_weight, preferred_element_type=jnp.float32).astype(jnp.bfloat16)
        query_heads = queries.reshape(TOKENS, H, HD).astype(jnp.float32)
        key_heads = image_keys.reshape(P_SIZE, H, HD).astype(jnp.float32)
        value_heads = image_values.reshape(P_SIZE, H, HD).astype(jnp.float32)
        grad_heads = image_grad.reshape(TOKENS, H, HD).astype(jnp.float32)
        scores = jnp.einsum("thd,phd->thp", query_heads, key_heads, precision=best) * score_scale
        visible = (phrase_ids[None, :] < count) & (first_block[None, :] <= block_ids[:, None]) & (block_ids[:, None] <= last_block[None, :])
        scores = jnp.where(visible[:, None, :], scores, -jnp.inf)
        row_max = jnp.max(scores, axis=-1, keepdims=True)
        exponent = jnp.exp(scores - row_max)
        attn_probs = exponent / jnp.sum(exponent, axis=-1, keepdims=True)
        probs_low = attn_probs.astype(jnp.bfloat16)
        prob_grad = jnp.einsum("thd,phd->thp", grad_heads, value_heads, precision=best)
        inner_sum = jnp.sum(attn_probs * prob_grad, axis=-1, keepdims=True)
        score_grad = (attn_probs * (prob_grad - inner_sum) * score_scale).astype(jnp.bfloat16)
        score_wide = score_grad.astype(jnp.float32)
        query_grad = jnp.einsum("thp,phd->thd", score_wide, key_heads, precision=best).astype(jnp.bfloat16).reshape(TOKENS, D)
        latent_grad = jnp.dot(query_grad, query_weight.T, preferred_element_type=jnp.float32).astype(jnp.bfloat16)
        key_grad = jnp.einsum("thp,thd->phd", score_wide, query_heads, precision=best).reshape(P_SIZE, D)
        value_grad = jnp.einsum("thp,thd->phd", probs_low.astype(jnp.float32), grad_heads, precision=best).reshape(P_SIZE, D)
        return latent_grad, key_grad, value_grad

    latent_grad, key_grad, value_grad = lax.map(one_image, (latents, out_grad, key_rows.reshape(IMAGES, P_SIZE, D), value_rows.reshape(IMAGES, P_SIZE, D), region_first, region_last, phrase_counts))
    key_low = key_grad.reshape(IMAGES * P_SIZE, D).astype(jnp.bfloat16)
    value_low = value_grad.reshape(IMAGES * P_SIZE, D).astype(jnp.bfloat16)
    encoded_grad = (jnp.dot(key_low, key_weight.T, preferred_element_type=jnp.float32) + jnp.dot(value_low, value_weight.T, preferred_element_type=jnp.float32)).astype(jnp.bfloat16)
    second_grad = jnp.dot(hidden.T, encoded_grad, preferred_element_type=jnp.float32)
    hidden_grad = jnp.dot(encoded_grad, second_weight.T, preferred_element_type=jnp.float32)
    act_grad = (hidden_grad * silu_slope(pre_act)).astype(jnp.bfloat16)
    first_grad = jnp.dot(phrase_rows.T, act_grad, preferred_element_type=jnp.float32)
    phrase_grad = jnp.dot(act_grad, first_weight.T, preferred_element_type=jnp.float32).astype(jnp.bfloat16).reshape(IMAGES, P_SIZE, D)
    return latent_grad, phrase_grad, first_grad, second_grad
```

```python
import jax
import jax.numpy as jnp
from jax import lax
from jax.experimental import pallas as pl
from jax.experimental.pallas import tpu as pltpu
from jax.sharding import PartitionSpec as P

MESH = pl.DeviceIdType.MESH
BF16 = jnp.bfloat16
F32 = jnp.float32
D = 1152
HD = 72
NP = 32
NS = 32
NZ = 8
NJ = 9
CB = 128
SR = D // NS
SRP = 40
TOK = 512
WIN = 640
SCALE = HD ** (-0.5)


def dot_nn(a, b):
    return lax.dot_general(a, b, (((1,), (0,)), ((), ())), preferred_element_type=F32)


def dot_nt(a, b):
    return lax.dot_general(a, b, (((1,), (1,)), ((), ())), preferred_element_type=F32)


def dot_tn(a, b):
    return lax.dot_general(a, b, (((0,), (0,)), ((), ())), preferred_element_type=F32)


def cols(j):
    return pl.ds(pl.multiple_of(j * CB, CB), CB)


def kernel(
    first_ref, last_ref, count_ref,
    lat_hbm, og_hbm, wq_hbm, phr_ref, w1_ref, w2_ref, wk_ref, wv_ref,
    lg_hbm, pg_ref, fg_ref, sg_ref,
    x_s, g_s, wq_s, q_s, qg_s, l_s,
    wbuf, w_f32, wc,
    hid_src, hid_s, enc_s, kv_src, kv_s, pre_s,
    kbd_s, vbd_s, st_s, pt_s, pr_s, sg_s, kvp_s,
    b1_s, part_s, rs_s,
    eg_src, eg_s, ag_src, ag_s, pgsrc_s, pgf_s,
    hc_s, pc_s, gz_s, zr_s, zf_s,
    ld_sem, out_sem,
    wsend, wrecv, hsend, hrecv, esend, erecv, kvsend, kvrecv,
    b1send, b1recv, rssend, rsrecv, egsend, egrecv, agsend, agrecv, pgsend, pgrecv,
    zsend, zrecv, zasend, zarecv,
):
    d = lax.axis_index("dp")
    s = lax.axis_index("seq")
    my_i = s // 16
    my_j = lax.rem(s, 16)
    is_w = my_j < NJ
    w_refs = (w1_ref, w2_ref, wk_ref, wv_ref)

    def seq_of(i, j):
        return i * 16 + j

    def remote(src, dst, ssem, rsem, dd, ss):
        pltpu.make_async_remote_copy(
            src_ref=src, dst_ref=dst, send_sem=ssem, recv_sem=rsem,
            device_id=(dd, ss), device_id_type=MESH,
        ).start()

    def wait_bytes(ref, sem):
        pltpu.make_async_copy(ref, ref, sem).wait()

    loads = [
        pltpu.make_async_copy(lat_hbm, x_s, ld_sem.at[0]),
        pltpu.make_async_copy(wq_hbm, wq_s, ld_sem.at[1]),
        pltpu.make_async_copy(og_hbm, g_s, ld_sem.at[2]),
    ]
    for load in loads:
        load.start()

    barrier = pltpu.get_barrier_semaphore()

    def sig_seq(k, c):
        pl.semaphore_signal(barrier, inc=1, device_id=(d, lax.rem(s + k, NS)), device_id_type=MESH)
        return c

    def sig_dp(k, c):
        pl.semaphore_signal(barrier, inc=1, device_id=(lax.rem(d + k, NZ), s), device_id_type=MESH)
        return c

    lax.fori_loop(1, NS, sig_seq, 0)
    lax.fori_loop(1, NZ, sig_dp, 0)
    pl.semaphore_wait(barrier, NS - 1 + NZ - 1)

    for w in range(4):
        def send_w(n, c, w=w):
            t = seq_of(n // NJ, lax.rem(n, NJ))
            j = lax.rem(n, NJ)

            @pl.when(t != s)
            def _():
                remote(w_refs[w].at[:, cols(j)], wbuf.at[w, s], wsend.at[w], wrecv.at[w], d, t)

            return c

        lax.fori_loop(0, 2 * NJ, send_w, 0)

    @pl.when(is_w)
    def _():
        for w in range(4):
            wbuf[w, s] = w_refs[w][:, cols(my_j)]

    sel = (
        lax.broadcasted_iota(jnp.int32, (SRP, D), 1)
        == lax.broadcasted_iota(jnp.int32, (SRP, D), 0) + s * SR
    ) & (lax.broadcasted_iota(jnp.int32, (SRP, D), 0) < SR)
    sel = jnp.where(sel, 1.0, 0.0).astype(BF16)
    for i in range(2):
        pc_s[i] = dot_nt(sel, phr_ref[i]).astype(BF16)

    def q_proj(i):
        def body(n, c):
            w = pl.ds(pl.multiple_of(n * 384, 128), 384)
            q_s[i, :, w] = dot_nn(x_s[i], wq_s[:, w]).astype(BF16)
            return c

        lax.fori_loop(0, 3, body, 0)

    def compact(w):
        for p in range(NS):
            w_f32[p * SR : (p + 1) * SR, :] = wbuf[w, p].astype(F32)
        wc[w] = w_f32[...].astype(BF16)

    def to_co_workers(src, dst, ssem, rsem):
        def body(jj, c):
            @pl.when(jj != my_j)
            def _():
                remote(src, dst, ssem, rsem, d, seq_of(my_i, jj))

            return c

        lax.fori_loop(0, NJ, body, 0)

    def to_plane(src, dst, ssem, rsem):
        def body(k, c):
            remote(src, dst, ssem, rsem, d, lax.rem(s + k, NS))
            return c

        lax.fori_loop(1, NS, body, 0)

    loads[0].wait()
    loads[1].wait()
    q_proj(0)

    @pl.when(is_w)
    def _():
        wait_bytes(wbuf.at[0, pl.ds(0, NS - 1)], wrecv.at[0])
        compact(0)
        pre = dot_nn(phr_ref[my_i], wc[0])
        pre_s[...] = pre
        hid = (pre / (1.0 + jnp.exp(-pre))).astype(BF16)
        hid_src[...] = hid
        hid_s[my_i, :, cols(my_j)] = hid
        to_co_workers(hid_src, hid_s.at[my_i, :, cols(my_j)], hsend.at[0], hrecv.at[my_i])

    q_proj(1)

    @pl.when(is_w)
    def _():
        wait_bytes(wbuf.at[1, pl.ds(0, NS - 1)], wrecv.at[1])
        compact(1)
        wait_bytes(rs_s.at[0, pl.ds(0, NJ - 1), pl.ds(0, NP // 2)], hrecv.at[my_i])
        enc = dot_nn(hid_s[my_i], wc[1]).astype(BF16)
        enc_s[:, cols(my_j)] = enc
        to_co_workers(enc_s.at[:, cols(my_j)], enc_s.at[:, cols(my_j)], esend, erecv)

        def rest(k, c):
            t = lax.rem(s + k, NS)

            @pl.when((t // 16 != my_i) | (lax.rem(t, 16) >= NJ))
            def _():
                remote(hid_src, hid_s.at[my_i, :, cols(my_j)], hsend.at[1], hrecv.at[my_i], d, t)

            return c

        lax.fori_loop(1, NS, rest, 0)
        for w in (2, 3):
            wait_bytes(wbuf.at[w, pl.ds(0, NS - 1)], wrecv.at[w])
            compact(w)
        wait_bytes(rs_s.at[0, pl.ds(0, NJ - 1), pl.ds(0, NP // 2)], erecv)
        enc_all = enc_s[...]
        kv_src[0:NP] = dot_nn(enc_all, wc[2]).astype(BF16)
        kv_src[NP : 2 * NP] = dot_nn(enc_all, wc[3]).astype(BF16)
        kv_s[my_i, :, cols(my_j)] = kv_src[...]
        to_plane(kv_src, kv_s.at[my_i, :, cols(my_j)], kvsend, kvrecv.at[my_i])

    def wait_blocks(ref9, ref8, sem, i):
        mine = is_w & (my_i == i)

        @pl.when(mine)
        def _():
            wait_bytes(ref8, sem)

        @pl.when(jnp.logical_not(mine))
        def _():
            wait_bytes(ref9, sem)

    loads[2].wait()
    sub8 = lax.broadcasted_iota(jnp.int32, (8, WIN), 0)
    lane = lax.broadcasted_iota(jnp.int32, (8, WIN), 1)

    def attention(i):
        wait_blocks(
            b1_s.at[pl.ds(0, NJ), pl.ds(0, NP)], b1_s.at[pl.ds(0, NJ - 1), pl.ds(0, NP)],
            kvrecv.at[i], i,
        )
        for g in range(2):
            lo = 512 * g
            off = lane + (lo - 576 * g) - sub8 * HD
            own = jnp.where((off >= 0) & (off < HD), 1.0, 0.0)
            keys = kv_s[i, 0:NP, lo : lo + WIN].astype(F32)
            vals = kv_s[i, NP : 2 * NP, lo : lo + WIN].astype(F32)
            kbd_s[i, g] = (keys[:, None, :] * own[None]).reshape(8 * NP, WIN).astype(BF16)
            vbd_s[...] = (vals[:, None, :] * own[None]).reshape(8 * NP, WIN).astype(BF16)
            st_s[...] = dot_nt(kbd_s[i, g], q_s[i, :, lo : lo + WIN])
            pt_s[...] = dot_nt(vbd_s[...], g_s[i, :, lo : lo + WIN])

            def block(b, c):
                tok = cols(b)
                blk = s * 4 + b
                sc = []
                for p in range(NP):
                    vis = (p < count_ref[i]) & (first_ref[i, p] <= blk) & (blk <= last_ref[i, p])
                    sc.append(jnp.where(vis, st_s[8 * p : 8 * p + 8, tok] * SCALE, -jnp.inf))

                def tree(op, vals):
                    while len(vals) > 1:
                        vals = [op(*vals[k : k + 2]) if k + 1 < len(vals) else vals[k] for k in range(0, len(vals), 2)]
                    return vals[0]

                top = tree(jnp.maximum, sc)
                ex = [jnp.exp(v - top) for v in sc]
                inv = 1.0 / tree(jnp.add, ex)
                pr = [e * inv for e in ex]
                for p in range(0, NP, 2):
                    pr_s[8 * p : 8 * p + 16, tok] = jnp.concatenate([pr[p], pr[p + 1]], axis=0).astype(BF16)
                pg = [pt_s[8 * p : 8 * p + 8, tok] for p in range(NP)]
                inner = tree(jnp.add, [pr[p] * pg[p] for p in range(NP)])
                for p in range(0, NP, 2):
                    sg_s[i, g, 8 * p : 8 * p + 16, tok] = jnp.concatenate(
                        [pr[q] * (pg[q] - inner) * SCALE for q in (p, p + 1)], axis=0
                    ).astype(BF16)
                return c

            lax.fori_loop(0, 4, block, 0)
            kp = dot_nn(sg_s[i, g], q_s[i, :, lo : lo + WIN])
            vp = dot_nn(pr_s[...], g_s[i, :, lo : lo + WIN])
            kp = jnp.sum(kp.reshape(NP, 8, WIN) * own[None], axis=1)
            vp = jnp.sum(vp.reshape(NP, 8, WIN) * own[None], axis=1)
            both = jnp.concatenate([kp, vp], axis=0)
            if g == 0:
                kvp_s[i, :, 0:WIN] = both
            else:
                kvp_s[i, :, lo:WIN] = kvp_s[i, :, lo:WIN] + both[:, 0:CB]
                kvp_s[i, :, WIN:D] = both[:, CB:WIN]

        def send_part(jj, c):
            t = seq_of(i, jj)

            @pl.when(t != s)
            def _():
                remote(kvp_s.at[i, :, cols(jj)], b1_s.at[s], b1send, b1recv, d, t)

            return c

        lax.fori_loop(0, NJ, send_part, 0)

    for i in range(2):
        attention(i)

    def query_grad(i):
        a0 = dot_tn(sg_s[i, 0], kbd_s[i, 0])
        a1 = dot_tn(sg_s[i, 1], kbd_s[i, 1])
        qg_s[i, :, 0:512] = a0[:, 0:512].astype(BF16)
        qg_s[i, :, 512:WIN] = (a0[:, 512:WIN] + a1[:, 0:CB]).astype(BF16)
        qg_s[i, :, WIN:D] = a1[:, CB:WIN].astype(BF16)

    def latent(i):
        def body(n, c):
            w = pl.ds(pl.multiple_of(n * 384, 128), 384)
            l_s[i, :, w] = dot_nt(qg_s[i], wq_s[w, :]).astype(BF16)
            return c

        lax.fori_loop(0, 3, body, 0)
        pltpu.make_async_copy(l_s.at[i], lg_hbm.at[i], out_sem.at[i]).start()

    for i in range(2):
        query_grad(i)
    latent(0)

    for i in range(2):
        mine = is_w & (my_i == i)

        @pl.when(jnp.logical_not(mine))
        def _():
            wait_bytes(rs_s.at[0, :, pl.ds(0, NP // 2)], hrecv.at[i])

    for i in range(2):
        hc_s[i] = dot_nt(sel, hid_s[i]).astype(BF16)

    def scatter_sum(n):
        def body(jj, c):
            @pl.when(jj != my_j)
            def _():
                remote(
                    part_s.at[n, :, cols(jj)], rs_s.at[n, my_j], rssend.at[n], rsrecv.at[n],
                    d, seq_of(my_i, jj),
                )

            return c

        lax.fori_loop(0, NJ, body, 0)
        rs_s[n, my_j] = part_s[n, :, cols(my_j)]

    def scatter_wait(n):
        wait_bytes(rs_s.at[n, pl.ds(0, NJ - 1)], rsrecv.at[n])
        total = rs_s[n, 0]
        for k in range(1, NJ):
            total = total + rs_s[n, k]
        return total

    @pl.when(is_w)
    def _():
        b1_s[s] = kvp_s[my_i, :, cols(my_j)]
        wait_bytes(b1_s.at[pl.ds(0, NS - 1)], b1recv)
        total = b1_s[0]
        for k in range(1, NS):
            total = total + b1_s[k]
        low = total.astype(BF16)
        part_s[0] = dot_nt(low[0:NP], wc[2]) + dot_nt(low[NP : 2 * NP], wc[3])
        scatter_sum(0)

    latent(1)

    @pl.when(is_w)
    def _():
        eg = scatter_wait(0).astype(BF16)
        part_s[1] = dot_nt(eg, wc[1])
        scatter_sum(1)
        eg_src[...] = eg
        eg_s[my_i, :, cols(my_j)] = eg
        to_plane(eg_src, eg_s.at[my_i, :, cols(my_j)], egsend, egrecv.at[my_i])
        hg = scatter_wait(1)
        pre = pre_s[...]
        sig = 1.0 / (1.0 + jnp.exp(-pre))
        ag = (hg * (sig * (1.0 + pre * (1.0 - sig)))).astype(BF16)
        ag_src[...] = ag
        ag_s[my_i, :, cols(my_j)] = ag
        to_plane(ag_src, ag_s.at[my_i, :, cols(my_j)], agsend, agrecv.at[my_i])
        part_s[2] = dot_nt(ag, wc[0])
        scatter_sum(2)

    def own8(n):
        return lax.rem(s, NZ)

    def z_scatter(k):
        def body(b, c):
            owner = jnp.where(b < NZ, b, own8(k))

            @pl.when(owner != d)
            def _():
                remote(gz_s.at[k, :, cols(b)], zr_s.at[k, b // NZ, d], zsend.at[k], zrecv.at[k, b // NZ], owner, s)

            return c

        lax.fori_loop(0, NJ, body, 0)
        zr_s[k, 0, d] = gz_s[k, :, cols(d)]

        @pl.when(own8(k) == d)
        def _():
            zr_s[k, 1, d] = gz_s[k, :, NZ * CB : D]

    def z_gather(k):
        def reduce(h, b):
            wait_bytes(zr_s.at[k, h, pl.ds(0, NZ - 1)], zrecv.at[k, h])
            total = zr_s[k, h, 0]
            for n in range(1, NZ):
                total = total + zr_s[k, h, n]
            zf_s[k, :, cols(b)] = total

            def body(n, c):
                remote(zf_s.at[k, :, cols(b)], zf_s.at[k, :, cols(b)], zasend.at[k, h], zarecv.at[k], lax.rem(d + n, NZ), s)
                return c

            lax.fori_loop(1, NZ, body, 0)

        reduce(0, d)

        @pl.when(own8(k) == d)
        def _():
            reduce(1, NZ)

    def z_finish(k, out):
        @pl.when(own8(k) == d)
        def _():
            wait_bytes(zr_s.at[k, 0, pl.ds(0, NZ - 1)], zarecv.at[k])

        @pl.when(own8(k) != d)
        def _():
            wait_bytes(zr_s.at[k, 0], zarecv.at[k])

        out[...] = zf_s[k, 0:SR, :]

    for i in range(2):
        wait_blocks(
            rs_s.at[0, :, pl.ds(0, NP // 2)], rs_s.at[0, pl.ds(0, NJ - 1), pl.ds(0, NP // 2)], egrecv.at[i], i
        )
    gz_s[0] = dot_nn(hc_s[0], eg_s[0]) + dot_nn(hc_s[1], eg_s[1])
    z_scatter(0)

    for i in range(2):
        wait_blocks(
            rs_s.at[0, :, pl.ds(0, NP // 2)], rs_s.at[0, pl.ds(0, NJ - 1), pl.ds(0, NP // 2)], agrecv.at[i], i
        )
    gz_s[1] = dot_nn(pc_s[0], ag_s[0]) + dot_nn(pc_s[1], ag_s[1])
    z_scatter(1)
    z_gather(0)

    @pl.when(is_w)
    def _():
        pgsrc_s[...] = scatter_wait(2).astype(BF16)
        pgf_s[my_i, :, cols(my_j)] = pgsrc_s[...]
        to_plane(pgsrc_s, pgf_s.at[my_i, :, cols(my_j)], pgsend, pgrecv.at[my_i])

    z_gather(1)
    z_finish(0, sg_ref)
    for i in range(2):
        wait_blocks(
            rs_s.at[0, :, pl.ds(0, NP // 2)], rs_s.at[0, pl.ds(0, NJ - 1), pl.ds(0, NP // 2)], pgrecv.at[i], i
        )
    pg_ref[...] = pgf_s[...]
    z_finish(1, fg_ref)

    for i in range(2):
        pltpu.make_async_copy(l_s.at[i], lg_hbm.at[i], out_sem.at[i]).wait()
    for w in range(4):
        @pl.when(is_w)
        def _():
            wait_bytes(wbuf.at[w, pl.ds(0, 2 * NJ - 1)], wsend.at[w])

        @pl.when(jnp.logical_not(is_w))
        def _():
            wait_bytes(wbuf.at[w, pl.ds(0, 2 * NJ)], wsend.at[w])

    @pl.when(is_w)
    def _():
        wait_bytes(b1_s.at[pl.ds(0, 2 * NJ - 1)], b1send)
        wait_bytes(rs_s.at[0, pl.ds(0, NJ - 1), pl.ds(0, NP // 2)], hsend.at[0])
        wait_bytes(b1_s.at[pl.ds(0, NS - NJ), pl.ds(0, NP // 2)], hsend.at[1])
        wait_bytes(rs_s.at[0, pl.ds(0, NJ - 1), pl.ds(0, NP // 2)], esend)
        wait_bytes(b1_s.at[pl.ds(0, NS - 1), pl.ds(0, NP)], kvsend)
        for n in range(3):
            wait_bytes(rs_s.at[n, pl.ds(0, NJ - 1)], rssend.at[n])
        for sem in (egsend, agsend, pgsend):
            wait_bytes(b1_s.at[pl.ds(0, NS - 1), pl.ds(0, NP // 2)], sem)

    @pl.when(jnp.logical_not(is_w))
    def _():
        wait_bytes(b1_s.at[pl.ds(0, 2 * NJ)], b1send)

    for k in range(2):
        @pl.when(own8(k) == d)
        def _():
            wait_bytes(zr_s.at[k, 0, pl.ds(0, NZ - 1)], zsend.at[k])
            wait_bytes(zr_s.at[k, 0, pl.ds(0, NZ - 1)], zasend.at[k, 1])

        @pl.when(own8(k) != d)
        def _():
            wait_bytes(zr_s.at[k, 0], zsend.at[k])

        wait_bytes(zr_s.at[k, 0, pl.ds(0, NZ - 1)], zasend.at[k, 0])


def local(
    latents, out_grad, phrases, query_weight, key_weight, value_weight, first_weight, second_weight,
    region_first, region_last, phrase_counts,
):
    vmem = pl.BlockSpec(memory_space=pltpu.VMEM)
    smem = pl.BlockSpec(memory_space=pltpu.SMEM)
    anyspace = pl.BlockSpec(memory_space=pl.ANY)
    V = pltpu.VMEM
    DMA = pltpu.SemaphoreType.DMA
    scratch = [
        V((2, TOK, D), BF16), V((2, TOK, D), BF16), V((D, D), BF16), V((2, TOK, D), BF16), V((2, TOK, D), BF16),
        V((2, TOK, D), BF16),
        V((4, NS, SR, CB), BF16), V((D, CB), F32), V((4, D, CB), BF16),
        V((NP, CB), BF16), V((2, NP, D), BF16), V((NP, D), BF16), V((2 * NP, CB), BF16), V((2, 2 * NP, D), BF16),
        V((NP, CB), F32),
        V((2, 2, 8 * NP, WIN), BF16), V((8 * NP, WIN), BF16), V((8 * NP, TOK), F32), V((8 * NP, TOK), F32),
        V((8 * NP, TOK), BF16), V((2, 2, 8 * NP, TOK), BF16), V((2, 2 * NP, D), F32),
        V((NS, 2 * NP, CB), F32), V((3, NP, D), F32), V((3, NJ, NP, CB), F32),
        V((NP, CB), BF16), V((2, NP, D), BF16), V((NP, CB), BF16), V((2, NP, D), BF16), V((NP, CB), BF16),
        V((2, NP, D), BF16),
        V((2, SRP, NP), BF16), V((2, SRP, NP), BF16), V((2, SRP, D), F32), V((2, 2, NZ, SRP, CB), F32),
        V((2, SRP, D), F32),
        DMA((3,)), DMA((2,)),
        DMA((4,)), DMA((4,)), DMA((2,)), DMA((2,)), DMA(()), DMA(()), DMA(()), DMA((2,)),
        DMA(()), DMA(()), DMA((3,)), DMA((3,)), DMA(()), DMA((2,)), DMA(()), DMA((2,)), DMA(()), DMA((2,)),
        DMA((2,)), DMA((2, 2)), DMA((2, 2)), DMA((2,)),
    ]
    return pl.pallas_call(
        kernel,
        out_shape=(
            jax.ShapeDtypeStruct((2, TOK, D), BF16),
            jax.ShapeDtypeStruct((2, NP, D), BF16),
            jax.ShapeDtypeStruct((SR, D), F32),
            jax.ShapeDtypeStruct((SR, D), F32),
        ),
        in_specs=[smem] * 3 + [anyspace] * 3 + [vmem] * 5,
        out_specs=(anyspace, vmem, vmem, vmem),
        scratch_shapes=scratch,
        compiler_params=pltpu.CompilerParams(
            collective_id=0, has_side_effects=True, vmem_limit_bytes=48 * 2**20
        ),
    )(
        region_first, region_last, phrase_counts, latents, out_grad, query_weight, phrases,
        first_weight, second_weight, key_weight, value_weight,
    )


def solution(mesh):
    in_specs = (
        P("dp", "seq", None), P("dp", "seq", None), P("dp", None, None), P(),
        P("seq", None), P("seq", None), P("seq", None), P("seq", None),
        P("dp", None), P("dp", None), P("dp"),
    )
    out_specs = (P("dp", "seq", None), P("dp", None, None), P("seq", None), P("seq", None))
    return jax.shard_map(local, mesh=mesh, in_specs=in_specs, out_specs=out_specs, check_vma=False)
```

```python
import jax
import jax.numpy as jnp
from jax import lax
from jax.experimental import pallas as pl
from jax.experimental.pallas import tpu as pltpu
from jax.sharding import PartitionSpec as P

MESH = pl.DeviceIdType.MESH
BF16 = jnp.bfloat16
F32 = jnp.float32
D = 1152
HD = 72
NP = 32
NS = 32
NZ = 8
NJ = 9
CB = 128
SR = D // NS
SRP = 40
TOK = 512
WIN = 640
SCALE = HD ** (-0.5)


def dot_nn(a, b):
    return lax.dot_general(a, b, (((1,), (0,)), ((), ())), preferred_element_type=F32)


def dot_nt(a, b):
    return lax.dot_general(a, b, (((1,), (1,)), ((), ())), preferred_element_type=F32)


def dot_tn(a, b):
    return lax.dot_general(a, b, (((0,), (0,)), ((), ())), preferred_element_type=F32)


def cols(j):
    return pl.ds(pl.multiple_of(j * CB, CB), CB)


def where_worker(n):
    i, j = n // NJ, lax.rem(n, NJ)
    k = j // 2
    y = lax.rem(1 + 2 * i + jnp.where(k == 1, 3, jnp.where(k == 2, 1, 0)), 4)
    x = lax.rem(1 + 2 * i + jnp.where(k == 3, 3, jnp.where(k == 4, 1, 0)), 4)
    return (y * 4 + x) * 2 + lax.rem(j, 2)


def worker_at(t):
    y, x, c = t // 8, lax.rem(t // 2, 4), lax.rem(t, 2)

    def block(i):
        ry, rx = lax.rem(y + 7 - 2 * i, 4), lax.rem(x + 7 - 2 * i, 4)
        row = jnp.where(rx == 0, 0, jnp.where(rx == 3, 3, jnp.where(rx == 1, 4, 9)))
        col = jnp.where(ry == 3, 1, jnp.where(ry == 1, 2, 9))
        k = jnp.where(ry == 0, row, jnp.where(rx == 0, col, 9))
        return 2 * k + c

    j0, j1 = block(0), block(1)
    i = jnp.where(j0 < NJ, 0, 1)
    j = jnp.where(j0 < NJ, j0, j1)
    return i, j, j < NJ


def kernel(
    first_hbm, last_hbm, count_hbm,
    lat_hbm, og_hbm, wq_hbm, phr_hbm, w1_hbm, w2_hbm, wk_hbm, wv_hbm,
    l_ref, pg_ref, fg_ref, sg_ref,
    first_ref, last_ref, count_ref, phr_ref, w_s,
    x_s, g_s, wq_s, q_s, qg_s,
    wbuf, w_f32, wc,
    hid_src, hid_s, enc_s, kv_src, kv_s, pre_s,
    kbd_s, vbd_s, st_s, pt_s, pr_s, sg_s, kvp_s, pair_s,
    kvb_s, b1_s, part_s, rs_s,
    eg_src, eg_s, ag_src, ag_s, pgsrc_s, pgf_s,
    hc_s, pc_s, gz_s, zr_s, zf_s,
    ld_sem,
    wsend, wrecv, hsend, hrecv, esend, erecv, kvsend, kvrecv, fwsend, fwrecv, prsend, prrecv,
    b1send, b1recv, rssend, rsrecv, egsend, egrecv, agsend, agrecv, pgsend, pgrecv,
    zsend, zrecv, zasend, zarecv,
):
    d = lax.axis_index("dp")
    s = lax.axis_index("seq")
    chip, core = s // 2, lax.rem(s, 2)
    other = 1 - core
    mate = s + 1 - 2 * core
    my_i, my_j, is_w = worker_at(s)
    my_j = jnp.where(is_w, my_j, 0)

    def remote(src, dst, ssem, rsem, dd, ss):
        pltpu.make_async_remote_copy(
            src_ref=src, dst_ref=dst, send_sem=ssem, recv_sem=rsem,
            device_id=(dd, ss), device_id_type=MESH,
        ).start()

    def wait_bytes(ref, sem):
        pltpu.make_async_copy(ref, ref, sem).wait()

    barrier = pltpu.get_barrier_semaphore()

    def sig_seq(k, c):
        pl.semaphore_signal(barrier, inc=1, device_id=(d, lax.rem(s + k, NS)), device_id_type=MESH)
        return c

    def sig_dp(k, c):
        pl.semaphore_signal(barrier, inc=1, device_id=(lax.rem(d + k, NZ), s), device_id_type=MESH)
        return c

    lax.fori_loop(1, NS, sig_seq, 0)
    lax.fori_loop(1, NZ, sig_dp, 0)

    pairs = (
        (w1_hbm, w_s.at[0]), (w2_hbm, w_s.at[1]), (wk_hbm, w_s.at[2]), (wv_hbm, w_s.at[3]),
        (lat_hbm, x_s), (wq_hbm, wq_s), (phr_hbm, phr_ref), (og_hbm, g_s),
        (first_hbm, first_ref), (last_hbm, last_ref), (count_hbm, count_ref),
    )
    loads = [pltpu.make_async_copy(a, b, ld_sem.at[n]) for n, (a, b) in enumerate(pairs)]
    for load in loads:
        load.start()

    def q_proj(i):
        q_s[i] = dot_nn(x_s[i], wq_s[...]).astype(BF16)

    loads[4].wait()
    loads[5].wait()
    q_proj(0)
    for n in range(4):
        loads[n].wait()
    pl.semaphore_wait(barrier, NS - 1 + NZ - 1)

    def send_weight(w):
        def body(k, c):
            n = lax.rem(s + k, 2 * NJ)
            j = lax.rem(n, NJ)
            t = where_worker(n)

            @pl.when(t != s)
            def _():
                remote(w_s.at[w, :, cols(j)], wbuf.at[w, s], wsend.at[w], wrecv.at[w], d, t)

            return c

        lax.fori_loop(0, 2 * NJ, body, 0)

    send_weight(0)
    send_weight(1)

    @pl.when(is_w)
    def _():
        for w in range(4):
            wbuf[w, s] = w_s[w, :, cols(my_j)]

    loads[6].wait()
    sel = (
        lax.broadcasted_iota(jnp.int32, (SRP, D), 1)
        == lax.broadcasted_iota(jnp.int32, (SRP, D), 0) + s * SR
    ) & (lax.broadcasted_iota(jnp.int32, (SRP, D), 0) < SR)
    sel = jnp.where(sel, 1.0, 0.0).astype(BF16)
    for i in range(2):
        pc_s[i] = dot_nt(sel, phr_ref[i]).astype(BF16)
    q_proj(1)

    @pl.when(jnp.logical_not(is_w))
    def _():
        send_weight(2)
        send_weight(3)

    def compact(w):
        for p in range(NS):
            w_f32[p * SR : (p + 1) * SR, :] = wbuf[w, p].astype(F32)
        wc[w] = w_f32[...].astype(BF16)

    def to_co_workers(src, dst, ssem, rsem):
        def body(k, c):
            jj = lax.rem(my_j + k, NJ)
            remote(src, dst, ssem, rsem, d, where_worker(my_i * NJ + jj))
            return c

        lax.fori_loop(1, NJ, body, 0)

    def to_plane(src, dst, ssem, rsem):
        def body(k, c):
            remote(src, dst, ssem, rsem, d, lax.rem(s + k, NS))
            return c

        lax.fori_loop(1, NS, body, 0)

    def slabs_of(n):
        return rs_s.at[0, pl.ds(0, n), pl.ds(0, NP // 2)]

    def wide_s(n):
        return wc.at[0, pl.ds(0, n * NP)]

    @pl.when(is_w)
    def _():
        wait_bytes(wbuf.at[0, pl.ds(0, NS - 1)], wrecv.at[0])
        compact(0)
        pre = dot_nn(phr_ref[my_i], wc[0])
        pre_s[...] = pre
        hid = (pre / (1.0 + jnp.exp(-pre))).astype(BF16)
        hid_src[...] = hid
        hid_s[my_i, :, cols(my_j)] = hid
        to_co_workers(hid_src, hid_s.at[my_i, :, cols(my_j)], hsend.at[0], hrecv.at[my_i])
        send_weight(2)
        send_weight(3)
        wait_bytes(wbuf.at[1, pl.ds(0, NS - 1)], wrecv.at[1])
        compact(1)
        wait_bytes(slabs_of(NJ - 1), hrecv.at[my_i])
        enc = dot_nn(hid_s[my_i], wc[1]).astype(BF16)
        enc_s[:, cols(my_j)] = enc
        to_co_workers(enc_s.at[:, cols(my_j)], enc_s.at[:, cols(my_j)], esend, erecv)
        for w in (2, 3):
            wait_bytes(wbuf.at[w, pl.ds(0, NS - 1)], wrecv.at[w])
            compact(w)
        wait_bytes(slabs_of(NJ - 1), erecv)
        enc_all = enc_s[...]
        kv_src[0:NP] = dot_nn(enc_all, wc[2]).astype(BF16)
        kv_src[NP : 2 * NP] = dot_nn(enc_all, wc[3]).astype(BF16)

        def send_kv(k, c):
            t = 2 * lax.rem(chip + k, NS // 2) + my_i

            @pl.when(t != s)
            def _():
                remote(kv_src, kv_s.at[my_i, :, cols(my_j)], kvsend, kvrecv, d, t)

            return c

        lax.fori_loop(0, NS // 2, send_kv, 0)

        @pl.when(core == my_i)
        def _():
            kv_s[my_i, :, cols(my_j)] = kv_src[...]

        def rest(k, c):
            t = lax.rem(s + k, NS)
            ti, _, tw = worker_at(t)

            @pl.when(jnp.logical_not(tw) | (ti != my_i))
            def _():
                remote(hid_src, hid_s.at[my_i, :, cols(my_j)], hsend.at[1], hrecv.at[my_i], d, t)

            return c

        lax.fori_loop(1, NS, rest, 0)

    for n in range(7, 11):
        loads[n].wait()
    sub8 = lax.broadcasted_iota(jnp.int32, (8, WIN), 0)
    lane = lax.broadcasted_iota(jnp.int32, (8, WIN), 1)

    def attention(i):
        for g in range(2):
            lo = 512 * g
            off = lane + (lo - 576 * g) - sub8 * HD
            own = jnp.where((off >= 0) & (off < HD), 1.0, 0.0)
            keys = kv_s[i, 0:NP, lo : lo + WIN].astype(F32)
            vals = kv_s[i, NP : 2 * NP, lo : lo + WIN].astype(F32)
            kbd_s[i, g] = (keys[:, None, :] * own[None]).reshape(8 * NP, WIN).astype(BF16)
            vbd_s[...] = (vals[:, None, :] * own[None]).reshape(8 * NP, WIN).astype(BF16)
            st_s[...] = dot_nt(kbd_s[i, g], q_s[i, :, lo : lo + WIN])
            pt_s[...] = dot_nt(vbd_s[...], g_s[i, :, lo : lo + WIN])

            def block(b, c):
                tok = cols(b)
                blk = s * 4 + b
                sc = []
                for p in range(NP):
                    vis = (p < count_ref[i]) & (first_ref[i, p] <= blk) & (blk <= last_ref[i, p])
                    sc.append(jnp.where(vis, st_s[8 * p : 8 * p + 8, tok] * SCALE, -jnp.inf))

                def tree(op, vals):
                    while len(vals) > 1:
                        vals = [op(*vals[k : k + 2]) if k + 1 < len(vals) else vals[k] for k in range(0, len(vals), 2)]
                    return vals[0]

                top = tree(jnp.maximum, sc)
                ex = [jnp.exp(v - top) for v in sc]
                inv = 1.0 / tree(jnp.add, ex)
                pr = [e * inv for e in ex]
                for p in range(0, NP, 2):
                    pr_s[8 * p : 8 * p + 16, tok] = jnp.concatenate([pr[p], pr[p + 1]], axis=0).astype(BF16)
                pg = [pt_s[8 * p : 8 * p + 8, tok] for p in range(NP)]
                inner = tree(jnp.add, [pr[p] * pg[p] for p in range(NP)])
                for p in range(0, NP, 2):
                    sg_s[i, g, 8 * p : 8 * p + 16, tok] = jnp.concatenate(
                        [pr[q] * (pg[q] - inner) * SCALE for q in (p, p + 1)], axis=0
                    ).astype(BF16)
                return c

            lax.fori_loop(0, 4, block, 0)
            kp = dot_nn(sg_s[i, g], q_s[i, :, lo : lo + WIN])
            vp = dot_nn(pr_s[...], g_s[i, :, lo : lo + WIN])
            kp = jnp.sum(kp.reshape(NP, 8, WIN) * own[None], axis=1)
            vp = jnp.sum(vp.reshape(NP, 8, WIN) * own[None], axis=1)
            both = jnp.concatenate([kp, vp], axis=0)
            if g == 0:
                kvp_s[i, :, 0:WIN] = both
            else:
                kvp_s[i, :, lo:WIN] = kvp_s[i, :, lo:WIN] + both[:, 0:CB]
                kvp_s[i, :, WIN:D] = both[:, CB:WIN]

    direct = is_w & (my_i == core)

    @pl.when(direct)
    def _():
        wait_bytes(b1_s.at[pl.ds(0, NJ - 1)], kvrecv)

    @pl.when(jnp.logical_not(direct))
    def _():
        wait_bytes(b1_s.at[pl.ds(0, NJ)], kvrecv)

    remote(kv_s.at[core], kv_s.at[core], fwsend, fwrecv, d, mate)
    attention(core)
    remote(kvp_s.at[core], pair_s, prsend, prrecv, d, mate)
    wait_bytes(kv_s.at[other], fwrecv)
    attention(other)
    wait_bytes(pair_s, prrecv)
    kvb_s[...] = (kvp_s[other] + pair_s[...]).astype(BF16)

    def send_part(k, c):
        jj = lax.rem(chip + k, NJ)
        t = where_worker(other * NJ + jj)

        @pl.when(t != s)
        def _():
            remote(kvb_s.at[:, cols(jj)], b1_s.at[chip], b1send, b1recv, d, t)

        return c

    lax.fori_loop(0, NJ, send_part, 0)
    from_self = is_w & (my_i == other)

    def query_grad(i):
        a0 = dot_tn(sg_s[i, 0], kbd_s[i, 0])
        a1 = dot_tn(sg_s[i, 1], kbd_s[i, 1])
        qg_s[i, :, 0:512] = a0[:, 0:512].astype(BF16)
        qg_s[i, :, 512:WIN] = (a0[:, 512:WIN] + a1[:, 0:CB]).astype(BF16)
        qg_s[i, :, WIN:D] = a1[:, CB:WIN].astype(BF16)

    for i in range(2):
        query_grad(i)
        l_ref[i] = dot_nt(qg_s[i], wq_s[...]).astype(BF16)

    for i in range(2):
        @pl.when(jnp.logical_not(is_w & (my_i == i)))
        def _():
            wait_bytes(slabs_of(NJ), hrecv.at[i])

        hc_s[i] = dot_nt(sel, hid_s[i]).astype(BF16)

    def scatter_sum(n):
        def body(k, c):
            jj = lax.rem(my_j + k, NJ)
            remote(
                part_s.at[n, :, cols(jj)], rs_s.at[n, my_j], rssend.at[n], rsrecv.at[n],
                d, where_worker(my_i * NJ + jj),
            )
            return c

        lax.fori_loop(1, NJ, body, 0)
        rs_s[n, my_j] = part_s[n, :, cols(my_j)]

    def scatter_wait(n):
        wait_bytes(rs_s.at[n, pl.ds(0, NJ - 1)], rsrecv.at[n])
        total = rs_s[n, 0]
        for k in range(1, NJ):
            total = total + rs_s[n, k]
        return total

    @pl.when(is_w)
    def _():
        @pl.when(from_self)
        def _():
            b1_s[chip] = kvb_s[:, cols(my_j)]
            wait_bytes(b1_s.at[pl.ds(0, NS // 2 - 1)], b1recv)

        @pl.when(jnp.logical_not(from_self))
        def _():
            wait_bytes(b1_s, b1recv)

        total = b1_s[0].astype(F32)
        for k in range(1, NS // 2):
            total = total + b1_s[k].astype(F32)
        low = total.astype(BF16)
        part_s[0] = dot_nt(low[0:NP], wc[2]) + dot_nt(low[NP : 2 * NP], wc[3])
        scatter_sum(0)
        eg = scatter_wait(0).astype(BF16)
        part_s[1] = dot_nt(eg, wc[1])
        scatter_sum(1)
        eg_src[...] = eg
        eg_s[my_i, :, cols(my_j)] = eg
        to_plane(eg_src, eg_s.at[my_i, :, cols(my_j)], egsend, egrecv.at[my_i])
        pre = pre_s[...]
        sig = 1.0 / (1.0 + jnp.exp(-pre))
        slope = sig * (1.0 + pre * (1.0 - sig))
        ag = (scatter_wait(1) * slope).astype(BF16)
        ag_src[...] = ag
        ag_s[my_i, :, cols(my_j)] = ag
        to_plane(ag_src, ag_s.at[my_i, :, cols(my_j)], agsend, agrecv.at[my_i])
        part_s[2] = dot_nt(ag, wc[0])
        scatter_sum(2)

    def wait_blocks(sem, i):
        mine = is_w & (my_i == i)

        @pl.when(mine)
        def _():
            wait_bytes(slabs_of(NJ - 1), sem)

        @pl.when(jnp.logical_not(mine))
        def _():
            wait_bytes(slabs_of(NJ), sem)

    eighth = lax.rem(s, NZ)

    def z_scatter(k):
        def body(n, c):
            b = lax.rem(d + n, NZ)
            remote(gz_s.at[k, :, cols(b)], zr_s.at[k, 0, d], zsend.at[k], zrecv.at[k, 0], b, s)
            return c

        lax.fori_loop(1, NZ, body, 0)
        zr_s[k, 0, d] = gz_s[k, :, cols(d)]

        @pl.when(eighth == d)
        def _():
            zr_s[k, 1, d] = gz_s[k, :, NZ * CB : D]

        @pl.when(eighth != d)
        def _():
            remote(gz_s.at[k, :, pl.ds(NZ * CB, CB)], zr_s.at[k, 1, d], zsend.at[k], zrecv.at[k, 1], eighth, s)

    def z_gather(k):
        def reduce(h, b):
            wait_bytes(zr_s.at[k, h, pl.ds(0, NZ - 1)], zrecv.at[k, h])
            total = zr_s[k, h, 0].astype(F32)
            for n in range(1, NZ):
                total = total + zr_s[k, h, n].astype(F32)
            zf_s[k, :, cols(b)] = total.astype(BF16)

            def body(n, c):
                remote(zf_s.at[k, :, cols(b)], zf_s.at[k, :, cols(b)], zasend.at[k, h], zarecv.at[k], lax.rem(d + n, NZ), s)
                return c

            lax.fori_loop(1, NZ, body, 0)

        reduce(0, d)

        @pl.when(eighth == d)
        def _():
            reduce(1, NZ)

    def z_finish(k, out):
        @pl.when(eighth == d)
        def _():
            wait_bytes(zr_s.at[k, 0, pl.ds(0, NZ - 1)], zarecv.at[k])

        @pl.when(eighth != d)
        def _():
            wait_bytes(zr_s.at[k, 0], zarecv.at[k])

        out[...] = zf_s[k].astype(F32)[0:SR]

    for i in range(2):
        wait_blocks(egrecv.at[i], i)
    gz_s[0] = (dot_nn(hc_s[0], eg_s[0]) + dot_nn(hc_s[1], eg_s[1])).astype(BF16)
    z_scatter(0)

    for i in range(2):
        wait_blocks(agrecv.at[i], i)
    gz_s[1] = (dot_nn(pc_s[0], ag_s[0]) + dot_nn(pc_s[1], ag_s[1])).astype(BF16)
    z_scatter(1)

    @pl.when(is_w)
    def _():
        pgsrc_s[...] = scatter_wait(2).astype(BF16)
        pgf_s[my_i, :, cols(my_j)] = pgsrc_s[...]
        to_plane(pgsrc_s, pgf_s.at[my_i, :, cols(my_j)], pgsend, pgrecv.at[my_i])

    z_gather(0)
    z_gather(1)
    z_finish(0, sg_ref)
    for i in range(2):
        wait_blocks(pgrecv.at[i], i)
    pg_ref[...] = pgf_s[...]

    @pl.when(is_w)
    def _():
        for w in range(4):
            wait_bytes(wbuf.at[w, pl.ds(0, 2 * NJ - 1)], wsend.at[w])
        for sem in (hsend.at[0], esend):
            wait_bytes(slabs_of(NJ - 1), sem)
        for n in range(3):
            wait_bytes(rs_s.at[n, pl.ds(0, NJ - 1)], rssend.at[n])
        wait_bytes(wide_s(NS - NJ), hsend.at[1])
        for sem in (egsend, agsend, pgsend):
            wait_bytes(wide_s(NS - 1), sem)

        @pl.when(direct)
        def _():
            wait_bytes(b1_s.at[pl.ds(0, NS // 2 - 1)], kvsend)

        @pl.when(jnp.logical_not(direct))
        def _():
            wait_bytes(b1_s, kvsend)

    @pl.when(jnp.logical_not(is_w))
    def _():
        for w in range(4):
            wait_bytes(wbuf.at[w, pl.ds(0, 2 * NJ)], wsend.at[w])

    @pl.when(from_self)
    def _():
        wait_bytes(b1_s.at[pl.ds(0, NJ - 1)], b1send)

    @pl.when(jnp.logical_not(from_self))
    def _():
        wait_bytes(b1_s.at[pl.ds(0, NJ)], b1send)

    wait_bytes(kv_s.at[core], fwsend)
    wait_bytes(pair_s, prsend)
    for k in range(2):
        @pl.when(eighth == d)
        def _():
            wait_bytes(zr_s.at[k, 0, pl.ds(0, NZ - 1)], zsend.at[k])
            wait_bytes(zr_s.at[k, 0, pl.ds(0, NZ - 1)], zasend.at[k, 1])

        @pl.when(eighth != d)
        def _():
            wait_bytes(zr_s.at[k, 0], zsend.at[k])

        wait_bytes(zr_s.at[k, 0, pl.ds(0, NZ - 1)], zasend.at[k, 0])
    z_finish(1, fg_ref)


def local(
    latents, out_grad, phrases, query_weight, key_weight, value_weight, first_weight, second_weight,
    region_first, region_last, phrase_counts,
):
    vmem = pl.BlockSpec(memory_space=pltpu.VMEM)
    hbm = pl.BlockSpec(memory_space=pltpu.HBM)
    V = pltpu.VMEM
    I32 = jnp.int32
    DMA = pltpu.SemaphoreType.DMA
    scratch = [
        pltpu.SMEM((2, NP), I32), pltpu.SMEM((2, NP), I32), pltpu.SMEM((2,), I32),
        V((2, NP, D), BF16), V((4, SR, D), BF16),
        V((2, TOK, D), BF16), V((2, TOK, D), BF16), V((D, D), BF16), V((2, TOK, D), BF16), V((2, TOK, D), BF16),
        V((4, NS, SR, CB), BF16), V((D, CB), F32), V((4, D, CB), BF16),
        V((NP, CB), BF16), V((2, NP, D), BF16), V((NP, D), BF16), V((2 * NP, CB), BF16), V((2, 2 * NP, D), BF16),
        V((NP, CB), F32),
        V((2, 2, 8 * NP, WIN), BF16), V((8 * NP, WIN), BF16), V((8 * NP, TOK), F32), V((8 * NP, TOK), F32),
        V((8 * NP, TOK), BF16), V((2, 2, 8 * NP, TOK), BF16), V((2, 2 * NP, D), F32), V((2 * NP, D), F32),
        V((2 * NP, D), BF16), V((NS // 2, 2 * NP, CB), BF16), V((3, NP, D), F32), V((3, NJ, NP, CB), F32),
        V((NP, CB), BF16), V((2, NP, D), BF16), V((NP, CB), BF16), V((2, NP, D), BF16), V((NP, CB), BF16),
        V((2, NP, D), BF16),
        V((2, SRP, NP), BF16), V((2, SRP, NP), BF16), V((2, SRP, D), BF16), V((2, 2, NZ, SRP, CB), BF16),
        V((2, SRP, D), BF16),
        DMA((11,)),
        DMA((4,)), DMA((4,)), DMA((2,)), DMA((2,)), DMA(()), DMA(()), DMA(()), DMA(()), DMA(()), DMA(()), DMA(()), DMA(()),
        DMA(()), DMA(()), DMA((3,)), DMA((3,)), DMA(()), DMA((2,)), DMA(()), DMA((2,)), DMA(()), DMA((2,)),
        DMA((2,)), DMA((2, 2)), DMA((2, 2)), DMA((2,)),
    ]
    return pl.pallas_call(
        kernel,
        out_shape=(
            jax.ShapeDtypeStruct((2, TOK, D), BF16),
            jax.ShapeDtypeStruct((2, NP, D), BF16),
            jax.ShapeDtypeStruct((SR, D), F32),
            jax.ShapeDtypeStruct((SR, D), F32),
        ),
        in_specs=[hbm] * 11,
        out_specs=(vmem, vmem, vmem, vmem),
        scratch_shapes=scratch,
        compiler_params=pltpu.CompilerParams(
            collective_id=0, has_side_effects=True, vmem_limit_bytes=48 * 2**20
        ),
    )(
        *[
            pltpu.with_memory_space_constraint(array, pltpu.HBM)
            for array in (
                region_first, region_last, phrase_counts, latents, out_grad, query_weight, phrases,
                first_weight, second_weight, key_weight, value_weight,
            )
        ]
    )


def solution(mesh):
    in_specs = (
        P("dp", "seq", None), P("dp", "seq", None), P("dp", None, None), P(),
        P("seq", None), P("seq", None), P("seq", None), P("seq", None),
        P("dp", None), P("dp", None), P("dp"),
    )
    out_specs = (P("dp", "seq", None), P("dp", None, None), P("seq", None), P("seq", None))
    return jax.shard_map(local, mesh=mesh, in_specs=in_specs, out_specs=out_specs, check_vma=False)
```

```python
import jax
import jax.numpy as jnp
from jax import lax
from jax.experimental import pallas as pl
from jax.experimental.pallas import tpu as pltpu
from jax.sharding import PartitionSpec as P

MESH = pl.DeviceIdType.MESH
BF16 = jnp.bfloat16
F32 = jnp.float32
D = 1152
HD = 72
NP = 32
NS = 32
NZ = 8
NJ = 9
CB = 128
SR = D // NS
SRP = 40
TOK = 512
WIN = 640
SCALE = HD ** (-0.5)


def dot_nn(a, b):
    return lax.dot_general(a, b, (((1,), (0,)), ((), ())), preferred_element_type=F32)


def dot_nt(a, b):
    return lax.dot_general(a, b, (((1,), (1,)), ((), ())), preferred_element_type=F32)


def dot_tn(a, b):
    return lax.dot_general(a, b, (((0,), (0,)), ((), ())), preferred_element_type=F32)


def cols(j):
    return pl.ds(pl.multiple_of(j * CB, CB), CB)


def where_worker(n):
    j = lax.rem(n, NJ)
    return 2 * (4 * (j // 3) + lax.rem(j, 3)) + n // NJ


def worker_at(t):
    y, x = t // 8, lax.rem(t // 2, 4)
    return lax.rem(t, 2), 3 * y + x, (x < 3) & (y < 3)


def kernel(
    first_hbm, last_hbm, count_hbm,
    lat_hbm, og_hbm, wq_hbm, phr_hbm, w1_hbm, w2_hbm, wk_hbm, wv_hbm,
    l_ref, pg_ref, fg_ref, sg_ref,
    first_ref, last_ref, count_ref, phr_ref, w_s,
    x_s, g_s, wq_s, q_s, qg_s,
    wbuf, w_f32, wc,
    hid_src, hid_s, enc_s, kv_src, kv_s, pre_s,
    kbd_s, vbd_s, st_s, pt_s, pr_s, sg_s, kvp_s, pair_s,
    kvb_s, b1_s, part_s, rs_s,
    eg_src, eg_s, ag_src, ag_s, pgsrc_s, pgf_s,
    hc_s, pc_s, gz_s, zr_s, zf_s,
    ld_sem,
    wsend, wrecv, swsend, swrecv, hsend, hrecv, esend, erecv, kvsend, kvrecv, fwsend, fwrecv, prsend, prrecv,
    b1send, b1recv, rssend, rsrecv, egsend, egrecv, agsend, agrecv, pgsend, pgrecv,
    zsend, zrecv, zasend, zarecv,
):
    d = lax.axis_index("dp")
    s = lax.axis_index("seq")
    chip, core = s // 2, lax.rem(s, 2)
    other = 1 - core
    mate = s + 1 - 2 * core
    my_i, my_j, is_w = worker_at(s)
    my_j = jnp.where(is_w, my_j, 0)

    def remote(src, dst, ssem, rsem, dd, ss):
        pltpu.make_async_remote_copy(
            src_ref=src, dst_ref=dst, send_sem=ssem, recv_sem=rsem,
            device_id=(dd, ss), device_id_type=MESH,
        ).start()

    def wait_bytes(ref, sem):
        pltpu.make_async_copy(ref, ref, sem).wait()

    barrier = pltpu.get_barrier_semaphore()

    def sig_seq(k, c):
        pl.semaphore_signal(barrier, inc=1, device_id=(d, lax.rem(s + k, NS)), device_id_type=MESH)
        return c

    def sig_dp(k, c):
        pl.semaphore_signal(barrier, inc=1, device_id=(lax.rem(d + k, NZ), s), device_id_type=MESH)
        return c

    lax.fori_loop(1, NS, sig_seq, 0)
    lax.fori_loop(1, NZ, sig_dp, 0)

    pairs = (
        (w1_hbm, w_s.at[0]), (w2_hbm, w_s.at[1]), (wk_hbm, w_s.at[2]), (wv_hbm, w_s.at[3]),
        (lat_hbm, x_s), (wq_hbm, wq_s), (phr_hbm, phr_ref), (og_hbm, g_s),
        (first_hbm, first_ref), (last_hbm, last_ref), (count_hbm, count_ref),
    )
    loads = [pltpu.make_async_copy(a, b, ld_sem.at[n]) for n, (a, b) in enumerate(pairs)]
    for load in loads:
        load.start()

    def q_proj(i):
        q_s[i] = dot_nn(x_s[i], wq_s[...]).astype(BF16)

    loads[4].wait()
    loads[5].wait()
    q_proj(0)
    for n in range(4):
        loads[n].wait()
    pl.semaphore_wait(barrier, NS - 1 + NZ - 1)

    half = NS // 2

    def send_weight(w):
        def body(k, c):
            j = lax.rem(chip + k, NJ)
            t = where_worker(core * NJ + j)

            @pl.when(t != s)
            def _():
                remote(w_s.at[w, :, cols(j)], wbuf.at[w, core * half + chip], wsend.at[w], wrecv.at[w], d, t)

            return c

        lax.fori_loop(0, NJ, body, 0)

    def swap_start(w):
        wait_bytes(wbuf.at[w, pl.ds(0, half - 1)], wrecv.at[w])
        got = wbuf.at[w, pl.ds(core * half, half)]
        remote(got, got, swsend.at[w], swrecv.at[w], d, mate)

    def swap_wait(w):
        wait_bytes(wbuf.at[w, pl.ds(0, half)], swrecv.at[w])

    send_weight(0)
    send_weight(1)

    @pl.when(is_w)
    def _():
        for w in range(4):
            wbuf[w, core * half + chip] = w_s[w, :, cols(my_j)]

    loads[6].wait()
    sel = (
        lax.broadcasted_iota(jnp.int32, (SRP, D), 1)
        == lax.broadcasted_iota(jnp.int32, (SRP, D), 0) + s * SR
    ) & (lax.broadcasted_iota(jnp.int32, (SRP, D), 0) < SR)
    sel = jnp.where(sel, 1.0, 0.0).astype(BF16)
    for i in range(2):
        pc_s[i] = dot_nt(sel, phr_ref[i]).astype(BF16)
    q_proj(1)

    @pl.when(jnp.logical_not(is_w))
    def _():
        send_weight(2)
        send_weight(3)

    def compact(w):
        for p in range(NS):
            w_f32[p * SR : (p + 1) * SR, :] = wbuf[w, (p % 2) * half + p // 2].astype(F32)
        wc[w] = w_f32[...].astype(BF16)

    def to_co_workers(src, dst, ssem, rsem):
        def body(k, c):
            jj = lax.rem(my_j + k, NJ)
            remote(src, dst, ssem, rsem, d, where_worker(my_i * NJ + jj))
            return c

        lax.fori_loop(1, NJ, body, 0)

    def to_plane(src, dst, ssem, rsem):
        def body(k, c):
            remote(src, dst, ssem, rsem, d, lax.rem(s + k, NS))
            return c

        lax.fori_loop(1, NS, body, 0)

    def slabs_of(n):
        return rs_s.at[0, pl.ds(0, n), pl.ds(0, NP // 2)]

    def wide_s(n):
        return wc.at[0, pl.ds(0, n * NP)]

    @pl.when(is_w)
    def _():
        swap_start(0)
        swap_wait(0)
        compact(0)
        pre = dot_nn(phr_ref[my_i], wc[0])
        pre_s[...] = pre
        hid = (pre / (1.0 + jnp.exp(-pre))).astype(BF16)
        hid_src[...] = hid
        hid_s[my_i, :, cols(my_j)] = hid
        to_co_workers(hid_src, hid_s.at[my_i, :, cols(my_j)], hsend.at[0], hrecv.at[my_i])
        send_weight(2)
        send_weight(3)
        swap_start(1)
        swap_wait(1)
        compact(1)
        wait_bytes(slabs_of(NJ - 1), hrecv.at[my_i])
        enc = dot_nn(hid_s[my_i], wc[1]).astype(BF16)
        enc_s[:, cols(my_j)] = enc
        to_co_workers(enc_s.at[:, cols(my_j)], enc_s.at[:, cols(my_j)], esend, erecv)
        for w in (2, 3):
            swap_start(w)
        for w in (2, 3):
            swap_wait(w)
            compact(w)
        wait_bytes(slabs_of(NJ - 1), erecv)
        enc_all = enc_s[...]
        kv_src[0:NP] = dot_nn(enc_all, wc[2]).astype(BF16)
        kv_src[NP : 2 * NP] = dot_nn(enc_all, wc[3]).astype(BF16)

        def send_kv(k, c):
            t = 2 * lax.rem(chip + k, NS // 2) + my_i

            @pl.when(t != s)
            def _():
                remote(kv_src, kv_s.at[my_i, :, cols(my_j)], kvsend, kvrecv, d, t)

            return c

        lax.fori_loop(0, NS // 2, send_kv, 0)

        @pl.when(core == my_i)
        def _():
            kv_s[my_i, :, cols(my_j)] = kv_src[...]

        def rest(k, c):
            t = lax.rem(s + k, NS)
            ti, _, tw = worker_at(t)

            @pl.when(jnp.logical_not(tw) | (ti != my_i))
            def _():
                remote(hid_src, hid_s.at[my_i, :, cols(my_j)], hsend.at[1], hrecv.at[my_i], d, t)

            return c

        lax.fori_loop(1, NS, rest, 0)

    for n in range(7, 11):
        loads[n].wait()
    sub8 = lax.broadcasted_iota(jnp.int32, (8, WIN), 0)
    lane = lax.broadcasted_iota(jnp.int32, (8, WIN), 1)

    def attention(i):
        for g in range(2):
            lo = 512 * g
            off = lane + (lo - 576 * g) - sub8 * HD
            own = jnp.where((off >= 0) & (off < HD), 1.0, 0.0)
            keys = kv_s[i, 0:NP, lo : lo + WIN].astype(F32)
            vals = kv_s[i, NP : 2 * NP, lo : lo + WIN].astype(F32)
            kbd_s[i, g] = (keys[:, None, :] * own[None]).reshape(8 * NP, WIN).astype(BF16)
            vbd_s[...] = (vals[:, None, :] * own[None]).reshape(8 * NP, WIN).astype(BF16)
            st_s[...] = dot_nt(kbd_s[i, g], q_s[i, :, lo : lo + WIN])
            pt_s[...] = dot_nt(vbd_s[...], g_s[i, :, lo : lo + WIN])

            def block(b, c):
                tok = cols(b)
                blk = s * 4 + b
                sc = []
                for p in range(NP):
                    vis = (p < count_ref[i]) & (first_ref[i, p] <= blk) & (blk <= last_ref[i, p])
                    sc.append(jnp.where(vis, st_s[8 * p : 8 * p + 8, tok] * SCALE, -jnp.inf))

                def tree(op, vals):
                    while len(vals) > 1:
                        vals = [op(*vals[k : k + 2]) if k + 1 < len(vals) else vals[k] for k in range(0, len(vals), 2)]
                    return vals[0]

                top = tree(jnp.maximum, sc)
                ex = [jnp.exp(v - top) for v in sc]
                inv = 1.0 / tree(jnp.add, ex)
                pr = [e * inv for e in ex]
                for p in range(0, NP, 2):
                    pr_s[8 * p : 8 * p + 16, tok] = jnp.concatenate([pr[p], pr[p + 1]], axis=0).astype(BF16)
                pg = [pt_s[8 * p : 8 * p + 8, tok] for p in range(NP)]
                inner = tree(jnp.add, [pr[p] * pg[p] for p in range(NP)])
                for p in range(0, NP, 2):
                    sg_s[i, g, 8 * p : 8 * p + 16, tok] = jnp.concatenate(
                        [pr[q] * (pg[q] - inner) * SCALE for q in (p, p + 1)], axis=0
                    ).astype(BF16)
                return c

            lax.fori_loop(0, 4, block, 0)
            kp = dot_nn(sg_s[i, g], q_s[i, :, lo : lo + WIN])
            vp = dot_nn(pr_s[...], g_s[i, :, lo : lo + WIN])
            kp = jnp.sum(kp.reshape(NP, 8, WIN) * own[None], axis=1)
            vp = jnp.sum(vp.reshape(NP, 8, WIN) * own[None], axis=1)
            both = jnp.concatenate([kp, vp], axis=0)
            if g == 0:
                kvp_s[i, :, 0:WIN] = both
            else:
                kvp_s[i, :, lo:WIN] = kvp_s[i, :, lo:WIN] + both[:, 0:CB]
                kvp_s[i, :, WIN:D] = both[:, CB:WIN]

    direct = is_w & (my_i == core)

    @pl.when(direct)
    def _():
        wait_bytes(b1_s.at[pl.ds(0, NJ - 1), pl.ds(0, NP)], kvrecv)

    @pl.when(jnp.logical_not(direct))
    def _():
        wait_bytes(b1_s.at[pl.ds(0, NJ), pl.ds(0, NP)], kvrecv)

    remote(kv_s.at[core], kv_s.at[core], fwsend, fwrecv, d, mate)
    attention(core)
    remote(kvp_s.at[core], pair_s, prsend, prrecv, d, mate)
    wait_bytes(kv_s.at[other], fwrecv)
    attention(other)
    wait_bytes(pair_s, prrecv)
    kvb_s[...] = kvp_s[other] + pair_s[...]

    def send_part(k, c):
        jj = lax.rem(chip + k, NJ)
        t = where_worker(other * NJ + jj)

        @pl.when(t != s)
        def _():
            remote(kvb_s.at[:, cols(jj)], b1_s.at[chip], b1send, b1recv, d, t)

        return c

    lax.fori_loop(0, NJ, send_part, 0)
    from_self = is_w & (my_i == other)

    def query_grad(i):
        a0 = dot_tn(sg_s[i, 0], kbd_s[i, 0])
        a1 = dot_tn(sg_s[i, 1], kbd_s[i, 1])
        qg_s[i, :, 0:512] = a0[:, 0:512].astype(BF16)
        qg_s[i, :, 512:WIN] = (a0[:, 512:WIN] + a1[:, 0:CB]).astype(BF16)
        qg_s[i, :, WIN:D] = a1[:, CB:WIN].astype(BF16)

    for i in range(2):
        query_grad(i)
        l_ref[i] = dot_nt(qg_s[i], wq_s[...]).astype(BF16)

    for i in range(2):
        @pl.when(jnp.logical_not(is_w & (my_i == i)))
        def _():
            wait_bytes(slabs_of(NJ), hrecv.at[i])

        hc_s[i] = dot_nt(sel, hid_s[i]).astype(BF16)

    def scatter_sum(n):
        def body(k, c):
            jj = lax.rem(my_j + k, NJ)
            remote(
                part_s.at[n, :, cols(jj)], rs_s.at[n, my_j], rssend.at[n], rsrecv.at[n],
                d, where_worker(my_i * NJ + jj),
            )
            return c

        lax.fori_loop(1, NJ, body, 0)
        rs_s[n, my_j] = part_s[n, :, cols(my_j)]

    def scatter_wait(n):
        wait_bytes(rs_s.at[n, pl.ds(0, NJ - 1)], rsrecv.at[n])
        total = rs_s[n, 0]
        for k in range(1, NJ):
            total = total + rs_s[n, k]
        return total

    @pl.when(is_w)
    def _():
        @pl.when(from_self)
        def _():
            b1_s[chip] = kvb_s[:, cols(my_j)]
            wait_bytes(b1_s.at[pl.ds(0, NS // 2 - 1)], b1recv)

        @pl.when(jnp.logical_not(from_self))
        def _():
            wait_bytes(b1_s, b1recv)

        total = b1_s[0]
        for k in range(1, NS // 2):
            total = total + b1_s[k]
        low = total.astype(BF16)
        part_s[0] = dot_nt(low[0:NP], wc[2]) + dot_nt(low[NP : 2 * NP], wc[3])
        scatter_sum(0)
        eg = scatter_wait(0).astype(BF16)
        part_s[1] = dot_nt(eg, wc[1])
        scatter_sum(1)
        eg_src[...] = eg
        eg_s[my_i, :, cols(my_j)] = eg
        to_plane(eg_src, eg_s.at[my_i, :, cols(my_j)], egsend, egrecv.at[my_i])
        pre = pre_s[...]
        sig = 1.0 / (1.0 + jnp.exp(-pre))
        slope = sig * (1.0 + pre * (1.0 - sig))
        ag = (scatter_wait(1) * slope).astype(BF16)
        ag_src[...] = ag
        ag_s[my_i, :, cols(my_j)] = ag
        to_plane(ag_src, ag_s.at[my_i, :, cols(my_j)], agsend, agrecv.at[my_i])
        part_s[2] = dot_nt(ag, wc[0])
        scatter_sum(2)

    def wait_blocks(sem, i):
        mine = is_w & (my_i == i)

        @pl.when(mine)
        def _():
            wait_bytes(slabs_of(NJ - 1), sem)

        @pl.when(jnp.logical_not(mine))
        def _():
            wait_bytes(slabs_of(NJ), sem)

    eighth = lax.rem(s, NZ)

    def z_scatter(k):
        def body(n, c):
            b = lax.rem(d + n, NZ)
            remote(gz_s.at[k, :, cols(b)], zr_s.at[k, 0, d], zsend.at[k], zrecv.at[k, 0], b, s)
            return c

        lax.fori_loop(1, NZ, body, 0)
        zr_s[k, 0, d] = gz_s[k, :, cols(d)]

        @pl.when(eighth == d)
        def _():
            zr_s[k, 1, d] = gz_s[k, :, NZ * CB : D]

        @pl.when(eighth != d)
        def _():
            remote(gz_s.at[k, :, pl.ds(NZ * CB, CB)], zr_s.at[k, 1, d], zsend.at[k], zrecv.at[k, 1], eighth, s)

    def z_gather(k):
        def reduce(h, b):
            wait_bytes(zr_s.at[k, h, pl.ds(0, NZ - 1)], zrecv.at[k, h])
            total = zr_s[k, h, 0].astype(F32)
            for n in range(1, NZ):
                total = total + zr_s[k, h, n].astype(F32)
            zf_s[k, :, cols(b)] = total.astype(BF16)

            def body(n, c):
                remote(zf_s.at[k, :, cols(b)], zf_s.at[k, :, cols(b)], zasend.at[k, h], zarecv.at[k], lax.rem(d + n, NZ), s)
                return c

            lax.fori_loop(1, NZ, body, 0)

        reduce(0, d)

        @pl.when(eighth == d)
        def _():
            reduce(1, NZ)

    def z_finish(k, out):
        @pl.when(eighth == d)
        def _():
            wait_bytes(zr_s.at[k, 0, pl.ds(0, NZ - 1)], zarecv.at[k])

        @pl.when(eighth != d)
        def _():
            wait_bytes(zr_s.at[k, 0], zarecv.at[k])

        out[...] = zf_s[k].astype(F32)[0:SR]

    for i in range(2):
        wait_blocks(egrecv.at[i], i)
    gz_s[0] = (dot_nn(hc_s[0], eg_s[0]) + dot_nn(hc_s[1], eg_s[1])).astype(BF16)
    z_scatter(0)

    for i in range(2):
        wait_blocks(agrecv.at[i], i)
    gz_s[1] = (dot_nn(pc_s[0], ag_s[0]) + dot_nn(pc_s[1], ag_s[1])).astype(BF16)
    z_scatter(1)

    @pl.when(is_w)
    def _():
        pgsrc_s[...] = scatter_wait(2).astype(BF16)
        pgf_s[my_i, :, cols(my_j)] = pgsrc_s[...]
        to_plane(pgsrc_s, pgf_s.at[my_i, :, cols(my_j)], pgsend, pgrecv.at[my_i])

    z_gather(0)
    z_gather(1)
    z_finish(0, sg_ref)
    for i in range(2):
        wait_blocks(pgrecv.at[i], i)
    pg_ref[...] = pgf_s[...]

    @pl.when(is_w)
    def _():
        for w in range(4):
            wait_bytes(wbuf.at[w, pl.ds(0, NJ - 1)], wsend.at[w])
            wait_bytes(wbuf.at[w, pl.ds(0, half)], swsend.at[w])
        for sem in (hsend.at[0], esend):
            wait_bytes(slabs_of(NJ - 1), sem)
        for n in range(3):
            wait_bytes(rs_s.at[n, pl.ds(0, NJ - 1)], rssend.at[n])
        wait_bytes(wide_s(NS - NJ), hsend.at[1])
        for sem in (egsend, agsend, pgsend):
            wait_bytes(wide_s(NS - 1), sem)

        @pl.when(direct)
        def _():
            wait_bytes(b1_s.at[pl.ds(0, NS // 2 - 1), pl.ds(0, NP)], kvsend)

        @pl.when(jnp.logical_not(direct))
        def _():
            wait_bytes(b1_s.at[:, pl.ds(0, NP)], kvsend)

    @pl.when(jnp.logical_not(is_w))
    def _():
        for w in range(4):
            wait_bytes(wbuf.at[w, pl.ds(0, NJ)], wsend.at[w])

    @pl.when(from_self)
    def _():
        wait_bytes(b1_s.at[pl.ds(0, NJ - 1)], b1send)

    @pl.when(jnp.logical_not(from_self))
    def _():
        wait_bytes(b1_s.at[pl.ds(0, NJ)], b1send)

    wait_bytes(kv_s.at[core], fwsend)
    wait_bytes(pair_s, prsend)
    for k in range(2):
        @pl.when(eighth == d)
        def _():
            wait_bytes(zr_s.at[k, 0, pl.ds(0, NZ - 1)], zsend.at[k])
            wait_bytes(zr_s.at[k, 0, pl.ds(0, NZ - 1)], zasend.at[k, 1])

        @pl.when(eighth != d)
        def _():
            wait_bytes(zr_s.at[k, 0], zsend.at[k])

        wait_bytes(zr_s.at[k, 0, pl.ds(0, NZ - 1)], zasend.at[k, 0])
    z_finish(1, fg_ref)


def local(
    latents, out_grad, phrases, query_weight, key_weight, value_weight, first_weight, second_weight,
    region_first, region_last, phrase_counts,
):
    vmem = pl.BlockSpec(memory_space=pltpu.VMEM)
    hbm = pl.BlockSpec(memory_space=pltpu.HBM)
    V = pltpu.VMEM
    I32 = jnp.int32
    DMA = pltpu.SemaphoreType.DMA
    scratch = [
        pltpu.SMEM((2, NP), I32), pltpu.SMEM((2, NP), I32), pltpu.SMEM((2,), I32),
        V((2, NP, D), BF16), V((4, SR, D), BF16),
        V((2, TOK, D), BF16), V((2, TOK, D), BF16), V((D, D), BF16), V((2, TOK, D), BF16), V((2, TOK, D), BF16),
        V((4, NS, SR, CB), BF16), V((D, CB), F32), V((4, D, CB), BF16),
        V((NP, CB), BF16), V((2, NP, D), BF16), V((NP, D), BF16), V((2 * NP, CB), BF16), V((2, 2 * NP, D), BF16),
        V((NP, CB), F32),
        V((2, 2, 8 * NP, WIN), BF16), V((8 * NP, WIN), BF16), V((8 * NP, TOK), F32), V((8 * NP, TOK), F32),
        V((8 * NP, TOK), BF16), V((2, 2, 8 * NP, TOK), BF16), V((2, 2 * NP, D), F32), V((2 * NP, D), F32),
        V((2 * NP, D), F32), V((NS // 2, 2 * NP, CB), F32), V((3, NP, D), F32), V((3, NJ, NP, CB), F32),
        V((NP, CB), BF16), V((2, NP, D), BF16), V((NP, CB), BF16), V((2, NP, D), BF16), V((NP, CB), BF16),
        V((2, NP, D), BF16),
        V((2, SRP, NP), BF16), V((2, SRP, NP), BF16), V((2, SRP, D), BF16), V((2, 2, NZ, SRP, CB), BF16),
        V((2, SRP, D), BF16),
        DMA((11,)),
        DMA((4,)), DMA((4,)), DMA((4,)), DMA((4,)), DMA((2,)), DMA((2,)), DMA(()), DMA(()), DMA(()), DMA(()), DMA(()), DMA(()), DMA(()), DMA(()),
        DMA(()), DMA(()), DMA((3,)), DMA((3,)), DMA(()), DMA((2,)), DMA(()), DMA((2,)), DMA(()), DMA((2,)),
        DMA((2,)), DMA((2, 2)), DMA((2, 2)), DMA((2,)),
    ]
    return pl.pallas_call(
        kernel,
        out_shape=(
            jax.ShapeDtypeStruct((2, TOK, D), BF16),
            jax.ShapeDtypeStruct((2, NP, D), BF16),
            jax.ShapeDtypeStruct((SR, D), F32),
            jax.ShapeDtypeStruct((SR, D), F32),
        ),
        in_specs=[hbm] * 11,
        out_specs=(vmem, vmem, vmem, vmem),
        scratch_shapes=scratch,
        compiler_params=pltpu.CompilerParams(
            collective_id=0, has_side_effects=True, vmem_limit_bytes=48 * 2**20
        ),
    )(
        *[
            pltpu.with_memory_space_constraint(array, pltpu.HBM)
            for array in (
                region_first, region_last, phrase_counts, latents, out_grad, query_weight, phrases,
                first_weight, second_weight, key_weight, value_weight,
            )
        ]
    )


def solution(mesh):
    in_specs = (
        P("dp", "seq", None), P("dp", "seq", None), P("dp", None, None), P(),
        P("seq", None), P("seq", None), P("seq", None), P("seq", None),
        P("dp", None), P("dp", None), P("dp"),
    )
    out_specs = (P("dp", "seq", None), P("dp", None, None), P("seq", None), P("seq", None))
    return jax.shard_map(local, mesh=mesh, in_specs=in_specs, out_specs=out_specs, check_vma=False)
```

```python
import jax
import jax.numpy as jnp
from jax import lax
from jax.experimental import pallas as pl
from jax.experimental.pallas import tpu as pltpu
from jax.sharding import PartitionSpec as P

MESH = pl.DeviceIdType.MESH
BF16 = jnp.bfloat16
F32 = jnp.float32
D = 1152
HD = 72
NP = 32
NS = 32
NZ = 8
NJ = 9
CB = 128
SR = D // NS
SRP = 40
TOK = 512
WIN = 640
SCALE = HD ** (-0.5)


def dot_nn(a, b):
    return lax.dot_general(a, b, (((1,), (0,)), ((), ())), preferred_element_type=F32)


def dot_nt(a, b):
    return lax.dot_general(a, b, (((1,), (1,)), ((), ())), preferred_element_type=F32)


def dot_tn(a, b):
    return lax.dot_general(a, b, (((0,), (0,)), ((), ())), preferred_element_type=F32)


def cols(j):
    return pl.ds(pl.multiple_of(j * CB, CB), CB)


def where_worker(n):
    j = lax.rem(n, NJ)
    return 2 * (4 * (j // 3) + lax.rem(j, 3)) + n // NJ


def worker_at(t):
    y, x = t // 8, lax.rem(t // 2, 4)
    return lax.rem(t, 2), 3 * y + x, (x < 3) & (y < 3)


def kernel(
    first_hbm, last_hbm, count_hbm,
    lat_hbm, og_hbm, wq_hbm, phr_hbm, w1_hbm, w2_hbm, wk_hbm, wv_hbm,
    l_ref, pg_ref, zf_s,
    first_ref, last_ref, count_ref, phr_ref, w_s,
    x_s, g_s, wq_s, q_s, qg_s,
    wbuf, w_f32, wc,
    hid_src, hid_s, enc_s, kv_src, kv_s, pre_s,
    kbd_s, vbd_s, st_s, pt_s, pr_s, sg_s, kvp_s, pair_s,
    kvb_s, b1_s, part_s, rs_s,
    eg_src, eg_s, ag_src, ag_s, pgsrc_s, pgf_s,
    hc_s, pc_s, gz_s, zr_s,
    ld_sem,
    wsend, wrecv, swsend, swrecv, hsend, hrecv, esend, erecv, kvsend, kvrecv, fwsend, fwrecv, prsend, prrecv,
    b1send, b1recv, rssend, rsrecv, egsend, egrecv, agsend, agrecv, pgsend, pgrecv,
    zsend, zrecv, zasend, zarecv,
):
    d = lax.axis_index("dp")
    s = lax.axis_index("seq")
    chip, core = s // 2, lax.rem(s, 2)
    other = 1 - core
    mate = s + 1 - 2 * core
    my_i, my_j, is_w = worker_at(s)
    my_j = jnp.where(is_w, my_j, 0)

    def remote(src, dst, ssem, rsem, dd, ss):
        pltpu.make_async_remote_copy(
            src_ref=src, dst_ref=dst, send_sem=ssem, recv_sem=rsem,
            device_id=(dd, ss), device_id_type=MESH,
        ).start()

    def wait_bytes(ref, sem):
        pltpu.make_async_copy(ref, ref, sem).wait()

    barrier = pltpu.get_barrier_semaphore()

    def sig_seq(k, c):
        pl.semaphore_signal(barrier, inc=1, device_id=(d, lax.rem(s + k, NS)), device_id_type=MESH)
        return c

    def sig_dp(k, c):
        pl.semaphore_signal(barrier, inc=1, device_id=(lax.rem(d + k, NZ), s), device_id_type=MESH)
        return c

    lax.fori_loop(1, NS, sig_seq, 0)
    lax.fori_loop(1, NZ, sig_dp, 0)

    pairs = (
        (w1_hbm, w_s.at[0]), (w2_hbm, w_s.at[1]), (wk_hbm, w_s.at[2]), (wv_hbm, w_s.at[3]),
        (lat_hbm, x_s), (wq_hbm, wq_s), (phr_hbm, phr_ref), (og_hbm, g_s),
        (first_hbm, first_ref), (last_hbm, last_ref), (count_hbm, count_ref),
    )
    loads = [pltpu.make_async_copy(a, b, ld_sem.at[n]) for n, (a, b) in enumerate(pairs)]
    for load in loads:
        load.start()

    def q_proj(i):
        q_s[i] = dot_nn(x_s[i], wq_s[...]).astype(BF16)

    loads[4].wait()
    loads[5].wait()
    q_proj(0)
    for n in range(4):
        loads[n].wait()
    pl.semaphore_wait(barrier, NS - 1 + NZ - 1)

    half = NS // 2

    def send_weight(w):
        def body(k, c):
            j = lax.rem(chip + k, NJ)
            t = where_worker(core * NJ + j)

            @pl.when(t != s)
            def _():
                remote(w_s.at[w, :, cols(j)], wbuf.at[w, core * half + chip], wsend.at[w], wrecv.at[w], d, t)

            return c

        lax.fori_loop(0, NJ, body, 0)

    def swap_start(w):
        wait_bytes(wbuf.at[w, pl.ds(0, half - 1)], wrecv.at[w])
        got = wbuf.at[w, pl.ds(core * half, half)]
        remote(got, got, swsend.at[w], swrecv.at[w], d, mate)

    def swap_wait(w):
        wait_bytes(wbuf.at[w, pl.ds(0, half)], swrecv.at[w])

    send_weight(0)
    send_weight(1)

    @pl.when(is_w)
    def _():
        for w in range(4):
            wbuf[w, core * half + chip] = w_s[w, :, cols(my_j)]

    loads[6].wait()
    sel = (
        lax.broadcasted_iota(jnp.int32, (SRP, D), 1)
        == lax.broadcasted_iota(jnp.int32, (SRP, D), 0) + s * SR
    ) & (lax.broadcasted_iota(jnp.int32, (SRP, D), 0) < SR)
    sel = jnp.where(sel, 1.0, 0.0).astype(BF16)
    for i in range(2):
        pc_s[i] = dot_nt(sel, phr_ref[i]).astype(BF16)
    q_proj(1)

    @pl.when(jnp.logical_not(is_w))
    def _():
        send_weight(2)
        send_weight(3)

    def compact(w):
        for p in range(NS):
            w_f32[p * SR : (p + 1) * SR, :] = wbuf[w, (p % 2) * half + p // 2].astype(F32)
        wc[w] = w_f32[...].astype(BF16)

    def to_co_workers(src, dst, ssem, rsem):
        def body(k, c):
            jj = lax.rem(my_j + k, NJ)
            remote(src, dst, ssem, rsem, d, where_worker(my_i * NJ + jj))
            return c

        lax.fori_loop(1, NJ, body, 0)

    def to_plane(src, dst, ssem, rsem):
        def body(k, c):
            remote(src, dst, ssem, rsem, d, lax.rem(s + k, NS))
            return c

        lax.fori_loop(1, NS, body, 0)

    def slabs_of(n):
        return rs_s.at[0, pl.ds(0, n), pl.ds(0, NP // 2)]

    def wide_s(n):
        return wc.at[0, pl.ds(0, n * NP)]

    @pl.when(is_w)
    def _():
        swap_start(0)
        swap_wait(0)
        compact(0)
        pre = dot_nn(phr_ref[my_i], wc[0])
        pre_s[...] = pre
        hid = (pre / (1.0 + jnp.exp(-pre))).astype(BF16)
        hid_src[...] = hid
        hid_s[my_i, :, cols(my_j)] = hid
        to_co_workers(hid_src, hid_s.at[my_i, :, cols(my_j)], hsend.at[0], hrecv.at[my_i])
        send_weight(2)
        send_weight(3)
        swap_start(1)
        swap_wait(1)
        compact(1)
        wait_bytes(slabs_of(NJ - 1), hrecv.at[my_i])
        enc = dot_nn(hid_s[my_i], wc[1]).astype(BF16)
        enc_s[:, cols(my_j)] = enc
        to_co_workers(enc_s.at[:, cols(my_j)], enc_s.at[:, cols(my_j)], esend, erecv)
        for w in (2, 3):
            swap_start(w)
        for w in (2, 3):
            swap_wait(w)
            compact(w)
        wait_bytes(slabs_of(NJ - 1), erecv)
        enc_all = enc_s[...]
        kv_src[0:NP] = dot_nn(enc_all, wc[2]).astype(BF16)
        kv_src[NP : 2 * NP] = dot_nn(enc_all, wc[3]).astype(BF16)

        def send_kv(k, c):
            t = 2 * lax.rem(chip + k, NS // 2) + my_i

            @pl.when(t != s)
            def _():
                remote(kv_src, kv_s.at[my_i, :, cols(my_j)], kvsend, kvrecv, d, t)

            return c

        lax.fori_loop(0, NS // 2, send_kv, 0)

        @pl.when(core == my_i)
        def _():
            kv_s[my_i, :, cols(my_j)] = kv_src[...]

        def rest(k, c):
            t = lax.rem(s + k, NS)
            ti, _, tw = worker_at(t)

            @pl.when(jnp.logical_not(tw) | (ti != my_i))
            def _():
                remote(hid_src, hid_s.at[my_i, :, cols(my_j)], hsend.at[1], hrecv.at[my_i], d, t)

            return c

        lax.fori_loop(1, NS, rest, 0)

    for n in range(7, 11):
        loads[n].wait()
    sub8 = lax.broadcasted_iota(jnp.int32, (8, WIN), 0)
    lane = lax.broadcasted_iota(jnp.int32, (8, WIN), 1)

    def attention(i):
        for g in range(2):
            lo = 512 * g
            off = lane + (lo - 576 * g) - sub8 * HD
            own = jnp.where((off >= 0) & (off < HD), 1.0, 0.0)
            keys = kv_s[i, 0:NP, lo : lo + WIN].astype(F32)
            vals = kv_s[i, NP : 2 * NP, lo : lo + WIN].astype(F32)
            kbd_s[i, g] = (keys[:, None, :] * own[None]).reshape(8 * NP, WIN).astype(BF16)
            vbd_s[...] = (vals[:, None, :] * own[None]).reshape(8 * NP, WIN).astype(BF16)
            st_s[...] = dot_nt(kbd_s[i, g], q_s[i, :, lo : lo + WIN])
            pt_s[...] = dot_nt(vbd_s[...], g_s[i, :, lo : lo + WIN])

            def block(b, c):
                tok = cols(b)
                blk = s * 4 + b
                sc = []
                for p in range(NP):
                    vis = (p < count_ref[i]) & (first_ref[i, p] <= blk) & (blk <= last_ref[i, p])
                    sc.append(jnp.where(vis, st_s[8 * p : 8 * p + 8, tok] * SCALE, -jnp.inf))

                def tree(op, vals):
                    while len(vals) > 1:
                        vals = [op(*vals[k : k + 2]) if k + 1 < len(vals) else vals[k] for k in range(0, len(vals), 2)]
                    return vals[0]

                top = tree(jnp.maximum, sc)
                ex = [jnp.exp(v - top) for v in sc]
                inv = 1.0 / tree(jnp.add, ex)
                pr = [e * inv for e in ex]
                for p in range(0, NP, 2):
                    pr_s[8 * p : 8 * p + 16, tok] = jnp.concatenate([pr[p], pr[p + 1]], axis=0).astype(BF16)
                pg = [pt_s[8 * p : 8 * p + 8, tok] for p in range(NP)]
                inner = tree(jnp.add, [pr[p] * pg[p] for p in range(NP)])
                for p in range(0, NP, 2):
                    sg_s[i, g, 8 * p : 8 * p + 16, tok] = jnp.concatenate(
                        [pr[q] * (pg[q] - inner) * SCALE for q in (p, p + 1)], axis=0
                    ).astype(BF16)
                return c

            lax.fori_loop(0, 4, block, 0)
            kp = dot_nn(sg_s[i, g], q_s[i, :, lo : lo + WIN])
            vp = dot_nn(pr_s[...], g_s[i, :, lo : lo + WIN])
            kp = jnp.sum(kp.reshape(NP, 8, WIN) * own[None], axis=1)
            vp = jnp.sum(vp.reshape(NP, 8, WIN) * own[None], axis=1)
            both = jnp.concatenate([kp, vp], axis=0)
            if g == 0:
                kvp_s[i, :, 0:WIN] = both
            else:
                kvp_s[i, :, lo:WIN] = kvp_s[i, :, lo:WIN] + both[:, 0:CB]
                kvp_s[i, :, WIN:D] = both[:, CB:WIN]

    direct = is_w & (my_i == core)

    @pl.when(direct)
    def _():
        wait_bytes(b1_s.at[pl.ds(0, NJ - 1), pl.ds(0, NP)], kvrecv)

    @pl.when(jnp.logical_not(direct))
    def _():
        wait_bytes(b1_s.at[pl.ds(0, NJ), pl.ds(0, NP)], kvrecv)

    remote(kv_s.at[core], kv_s.at[core], fwsend, fwrecv, d, mate)
    attention(core)
    remote(kvp_s.at[core], pair_s, prsend, prrecv, d, mate)
    wait_bytes(kv_s.at[other], fwrecv)
    attention(other)
    wait_bytes(pair_s, prrecv)
    kvb_s[...] = kvp_s[other] + pair_s[...]

    def send_part(k, c):
        jj = lax.rem(chip + k, NJ)
        t = where_worker(other * NJ + jj)

        @pl.when(t != s)
        def _():
            remote(kvb_s.at[:, cols(jj)], b1_s.at[chip], b1send, b1recv, d, t)

        return c

    lax.fori_loop(0, NJ, send_part, 0)
    from_self = is_w & (my_i == other)

    def query_grad(i):
        a0 = dot_tn(sg_s[i, 0], kbd_s[i, 0])
        a1 = dot_tn(sg_s[i, 1], kbd_s[i, 1])
        qg_s[i, :, 0:512] = a0[:, 0:512].astype(BF16)
        qg_s[i, :, 512:WIN] = (a0[:, 512:WIN] + a1[:, 0:CB]).astype(BF16)
        qg_s[i, :, WIN:D] = a1[:, CB:WIN].astype(BF16)

    for i in range(2):
        query_grad(i)
        l_ref[i] = dot_nt(qg_s[i], wq_s[...]).astype(BF16)

    for i in range(2):
        @pl.when(jnp.logical_not(is_w & (my_i == i)))
        def _():
            wait_bytes(slabs_of(NJ), hrecv.at[i])

        hc_s[i] = dot_nt(sel, hid_s[i]).astype(BF16)

    def scatter_sum(n):
        def body(k, c):
            jj = lax.rem(my_j + k, NJ)
            remote(
                part_s.at[n, :, cols(jj)], rs_s.at[n, my_j], rssend.at[n], rsrecv.at[n],
                d, where_worker(my_i * NJ + jj),
            )
            return c

        lax.fori_loop(1, NJ, body, 0)
        rs_s[n, my_j] = part_s[n, :, cols(my_j)]

    def scatter_wait(n):
        wait_bytes(rs_s.at[n, pl.ds(0, NJ - 1)], rsrecv.at[n])
        total = rs_s[n, 0]
        for k in range(1, NJ):
            total = total + rs_s[n, k]
        return total

    @pl.when(is_w)
    def _():
        @pl.when(from_self)
        def _():
            b1_s[chip] = kvb_s[:, cols(my_j)]
            wait_bytes(b1_s.at[pl.ds(0, NS // 2 - 1)], b1recv)

        @pl.when(jnp.logical_not(from_self))
        def _():
            wait_bytes(b1_s, b1recv)

        total = b1_s[0]
        for k in range(1, NS // 2):
            total = total + b1_s[k]
        low = total.astype(BF16)
        part_s[0] = dot_nt(low[0:NP], wc[2]) + dot_nt(low[NP : 2 * NP], wc[3])
        scatter_sum(0)
        eg = scatter_wait(0).astype(BF16)
        part_s[1] = dot_nt(eg, wc[1])
        scatter_sum(1)
        eg_src[...] = eg
        eg_s[my_i, :, cols(my_j)] = eg
        to_plane(eg_src, eg_s.at[my_i, :, cols(my_j)], egsend, egrecv.at[my_i])
        pre = pre_s[...]
        sig = 1.0 / (1.0 + jnp.exp(-pre))
        slope = sig * (1.0 + pre * (1.0 - sig))
        ag = (scatter_wait(1) * slope).astype(BF16)
        ag_src[...] = ag
        ag_s[my_i, :, cols(my_j)] = ag
        to_plane(ag_src, ag_s.at[my_i, :, cols(my_j)], agsend, agrecv.at[my_i])
        part_s[2] = dot_nt(ag, wc[0])
        scatter_sum(2)

    def wait_blocks(sem, i):
        mine = is_w & (my_i == i)

        @pl.when(mine)
        def _():
            wait_bytes(slabs_of(NJ - 1), sem)

        @pl.when(jnp.logical_not(mine))
        def _():
            wait_bytes(slabs_of(NJ), sem)

    eighth = lax.rem(s, NZ)

    def z_scatter(k):
        def body(n, c):
            b = lax.rem(d + n, NZ)
            remote(gz_s.at[k, :, cols(b)], zr_s.at[k, 0, d], zsend.at[k], zrecv.at[k, 0], b, s)
            return c

        lax.fori_loop(1, NZ, body, 0)
        zr_s[k, 0, d] = gz_s[k, :, cols(d)]

        @pl.when(eighth == d)
        def _():
            zr_s[k, 1, d] = gz_s[k, :, NZ * CB : D]

        @pl.when(eighth != d)
        def _():
            remote(gz_s.at[k, :, pl.ds(NZ * CB, CB)], zr_s.at[k, 1, d], zsend.at[k], zrecv.at[k, 1], eighth, s)

    def z_gather(k):
        def reduce(h, b):
            wait_bytes(zr_s.at[k, h, pl.ds(0, NZ - 1)], zrecv.at[k, h])
            total = zr_s[k, h, 0].astype(F32)
            for n in range(1, NZ):
                total = total + zr_s[k, h, n].astype(F32)
            zf_s[k, :, cols(b)] = total.astype(BF16)

            def body(n, c):
                remote(zf_s.at[k, :, cols(b)], zf_s.at[k, :, cols(b)], zasend.at[k, h], zarecv.at[k], lax.rem(d + n, NZ), s)
                return c

            lax.fori_loop(1, NZ, body, 0)

        reduce(0, d)

        @pl.when(eighth == d)
        def _():
            reduce(1, NZ)

    def z_finish(k):
        @pl.when(eighth == d)
        def _():
            wait_bytes(zr_s.at[k, 0, pl.ds(0, NZ - 1)], zarecv.at[k])

        @pl.when(eighth != d)
        def _():
            wait_bytes(zr_s.at[k, 0], zarecv.at[k])


    for i in range(2):
        wait_blocks(egrecv.at[i], i)
    gz_s[0] = (dot_nn(hc_s[0], eg_s[0]) + dot_nn(hc_s[1], eg_s[1])).astype(BF16)
    z_scatter(0)

    for i in range(2):
        wait_blocks(agrecv.at[i], i)
    gz_s[1] = (dot_nn(pc_s[0], ag_s[0]) + dot_nn(pc_s[1], ag_s[1])).astype(BF16)
    z_scatter(1)

    @pl.when(is_w)
    def _():
        pgsrc_s[...] = scatter_wait(2).astype(BF16)
        pgf_s[my_i, :, cols(my_j)] = pgsrc_s[...]
        to_plane(pgsrc_s, pgf_s.at[my_i, :, cols(my_j)], pgsend, pgrecv.at[my_i])

    z_gather(0)
    z_gather(1)
    z_finish(0)
    for i in range(2):
        wait_blocks(pgrecv.at[i], i)
    pg_ref[...] = pgf_s[...]

    @pl.when(is_w)
    def _():
        for w in range(4):
            wait_bytes(wbuf.at[w, pl.ds(0, NJ - 1)], wsend.at[w])
            wait_bytes(wbuf.at[w, pl.ds(0, half)], swsend.at[w])
        for sem in (hsend.at[0], esend):
            wait_bytes(slabs_of(NJ - 1), sem)
        for n in range(3):
            wait_bytes(rs_s.at[n, pl.ds(0, NJ - 1)], rssend.at[n])
        wait_bytes(wide_s(NS - NJ), hsend.at[1])
        for sem in (egsend, agsend, pgsend):
            wait_bytes(wide_s(NS - 1), sem)

        @pl.when(direct)
        def _():
            wait_bytes(b1_s.at[pl.ds(0, NS // 2 - 1), pl.ds(0, NP)], kvsend)

        @pl.when(jnp.logical_not(direct))
        def _():
            wait_bytes(b1_s.at[:, pl.ds(0, NP)], kvsend)

    @pl.when(jnp.logical_not(is_w))
    def _():
        for w in range(4):
            wait_bytes(wbuf.at[w, pl.ds(0, NJ)], wsend.at[w])

    @pl.when(from_self)
    def _():
        wait_bytes(b1_s.at[pl.ds(0, NJ - 1)], b1send)

    @pl.when(jnp.logical_not(from_self))
    def _():
        wait_bytes(b1_s.at[pl.ds(0, NJ)], b1send)

    wait_bytes(kv_s.at[core], fwsend)
    wait_bytes(pair_s, prsend)
    for k in range(2):
        @pl.when(eighth == d)
        def _():
            wait_bytes(zr_s.at[k, 0, pl.ds(0, NZ - 1)], zsend.at[k])
            wait_bytes(zr_s.at[k, 0, pl.ds(0, NZ - 1)], zasend.at[k, 1])

        @pl.when(eighth != d)
        def _():
            wait_bytes(zr_s.at[k, 0], zsend.at[k])

        wait_bytes(zr_s.at[k, 0, pl.ds(0, NZ - 1)], zasend.at[k, 0])
    z_finish(1)


def local(
    latents, out_grad, phrases, query_weight, key_weight, value_weight, first_weight, second_weight,
    region_first, region_last, phrase_counts,
):
    vmem = pl.BlockSpec(memory_space=pltpu.VMEM)
    hbm = pl.BlockSpec(memory_space=pltpu.HBM)
    V = pltpu.VMEM
    I32 = jnp.int32
    DMA = pltpu.SemaphoreType.DMA
    scratch = [
        pltpu.SMEM((2, NP), I32), pltpu.SMEM((2, NP), I32), pltpu.SMEM((2,), I32),
        V((2, NP, D), BF16), V((4, SR, D), BF16),
        V((2, TOK, D), BF16), V((2, TOK, D), BF16), V((D, D), BF16), V((2, TOK, D), BF16), V((2, TOK, D), BF16),
        V((4, NS, SR, CB), BF16), V((D, CB), F32), V((4, D, CB), BF16),
        V((NP, CB), BF16), V((2, NP, D), BF16), V((NP, D), BF16), V((2 * NP, CB), BF16), V((2, 2 * NP, D), BF16),
        V((NP, CB), F32),
        V((2, 2, 8 * NP, WIN), BF16), V((8 * NP, WIN), BF16), V((8 * NP, TOK), F32), V((8 * NP, TOK), F32),
        V((8 * NP, TOK), BF16), V((2, 2, 8 * NP, TOK), BF16), V((2, 2 * NP, D), F32), V((2 * NP, D), F32),
        V((2 * NP, D), F32), V((NS // 2, 2 * NP, CB), F32), V((3, NP, D), F32), V((3, NJ, NP, CB), F32),
        V((NP, CB), BF16), V((2, NP, D), BF16), V((NP, CB), BF16), V((2, NP, D), BF16), V((NP, CB), BF16),
        V((2, NP, D), BF16),
        V((2, SRP, NP), BF16), V((2, SRP, NP), BF16), V((2, SRP, D), BF16), V((2, 2, NZ, SRP, CB), BF16),
        DMA((11,)),
        DMA((4,)), DMA((4,)), DMA((4,)), DMA((4,)), DMA((2,)), DMA((2,)), DMA(()), DMA(()), DMA(()), DMA(()), DMA(()), DMA(()), DMA(()), DMA(()),
        DMA(()), DMA(()), DMA((3,)), DMA((3,)), DMA(()), DMA((2,)), DMA(()), DMA((2,)), DMA(()), DMA((2,)),
        DMA((2,)), DMA((2, 2)), DMA((2, 2)), DMA((2,)),
    ]
    latent_grad, phrase_grad, sums = pl.pallas_call(
        kernel,
        out_shape=(
            jax.ShapeDtypeStruct((2, TOK, D), BF16),
            jax.ShapeDtypeStruct((2, NP, D), BF16),
            jax.ShapeDtypeStruct((2, SRP, D), BF16),
        ),
        in_specs=[hbm] * 11,
        out_specs=(vmem, vmem, vmem),
        scratch_shapes=scratch,
        compiler_params=pltpu.CompilerParams(
            collective_id=0, has_side_effects=True, vmem_limit_bytes=48 * 2**20
        ),
    )(
        *[
            pltpu.with_memory_space_constraint(array, pltpu.HBM)
            for array in (
                region_first, region_last, phrase_counts, latents, out_grad, query_weight, phrases,
                first_weight, second_weight, key_weight, value_weight,
            )
        ]
    )
    return latent_grad, phrase_grad, sums[1, 0:SR].astype(F32), sums[0, 0:SR].astype(F32)


def solution(mesh):
    in_specs = (
        P("dp", "seq", None), P("dp", "seq", None), P("dp", None, None), P(),
        P("seq", None), P("seq", None), P("seq", None), P("seq", None),
        P("dp", None), P("dp", None), P("dp"),
    )
    out_specs = (P("dp", "seq", None), P("dp", None, None), P("seq", None), P("seq", None))
    return jax.shard_map(local, mesh=mesh, in_specs=in_specs, out_specs=out_specs, check_vma=False)
```
